256 devices in a mesh: dp: 16 (over y_lo, x, core), ctx: 16 (over y_hi, z).
Axes of the slice: x: 4, y: 4 (y_hi: 2, y_lo: 2; y = y_hi * 2 + y_lo), z: 8, core: 2. Of those that a mesh axis runs over, the one named last changes fastest.
Arguments:
- roll_query: bfloat16 [16, 2048, 4096], P('dp', 'ctx'), may hold values from -12 to 12
- roll_keys: bfloat16 [16, 2048, 512], P('dp', 'ctx'), may hold values from -12 to 12
- roll_values: bfloat16 [16, 2048, 512], P('dp', 'ctx'), may hold values from -6 to 6
- pack_dest: int32 [16, 256], P(None, 'ctx'), may hold values from 0 to 15, as said below
- segment_ids: int32 [16, 2048], P('dp', 'ctx'), may hold values from 0 to 15, never falling along the last dimension, each value on 1 to 1024 neighbouring positions
- reward_bins: int32 [16, 16], P('dp'), may hold values from 0 to 511
- reward_weight: float32 [4096], replicated, may hold values from -0.5 to 0.5
Outputs:
- attention_out: bfloat16 [16, 2048, 4096], P('dp', 'ctx')
- reward_hist: float32 [512], replicated
The draws below stay inside these ranges and needn't reach their ends.
Inputs may be any that keep to these rules, and one draw needn't show every extreme that they name: For every column j the entries pack_dest[s, j] over s are a permutation of the packed sequences. Among the 16 columns of one ctx shard, at most 1 block go from one source to one packed sequence, and exactly 1 for some pair in every shard.
All inputs are finite; a program needn't handle non-finite values.
Results may differ from the reference program's by a relative error of at most 0.004.
Values may be sent and summed in bfloat16 or wider, within the bound.
A program may use at most 64 MiB of HBM per device.

```python
import math
import jax
import jax.numpy as jnp
import numpy as np
from jax import lax

HQ = 32
HK = 4
HD = 128
TQ = 128
BLK = 8
SEGS = 16
BINS = 512
NB = 16
SEQ_LEN = 2048
SEQS = 16


def draw_roll_query(key, part):
    full_shape = (SEQS, SEQ_LEN, HQ * HD)
    values = jnp.clip(jax.random.normal(jax.random.fold_in(key, 7), full_shape, jnp.float32), -4.0, 4.0)
    return values.astype(jnp.bfloat16)


def draw_roll_keys(key, part):
    full_shape = (SEQS, SEQ_LEN, HK * HD)
    values = jnp.clip(jax.random.normal(jax.random.fold_in(key, 19), full_shape, jnp.float32), -4.0, 4.0)
    return values.astype(jnp.bfloat16)


def draw_pack_dest(key, part):
    ctx_count = SEQ_LEN // TQ
    cycle_len = min(NB, SEQS)

    def one_shard(shard_key):
        split_keys = jax.random.split(shard_key, 5)
        relabel = jax.random.permutation(split_keys[0], SEQS).astype(jnp.int32)
        start_map = jax.random.permutation(split_keys[1], SEQS).astype(jnp.int32)
        distinct = jax.random.permutation(split_keys[3], SEQS).astype(jnp.int32)
        block_ids = jnp.arange(NB, dtype=jnp.int32)
        picked = block_ids % cycle_len
        offsets = distinct[picked]
        offsets = offsets[jax.random.permutation(split_keys[4], NB)]
        return relabel[(start_map[:, None] + offsets[None, :]) % SEQS]
    shard_keys = jax.random.split(jax.random.fold_in(key, 29), ctx_count)
    tables = jax.vmap(one_shard)(shard_keys)
    return jnp.transpose(tables, (1, 0, 2)).reshape(SEQS, ctx_count * NB).astype(jnp.int32)


def with_ends(result, rng, low, top_value):
    place = [jax.random.randint(jax.random.fold_in(rng, axis), (), 0, length) for axis, length in enumerate(result.shape)]
    longest = result.shape.index(max(result.shape))
    neighbour = place[:longest] + [(place[longest] + 1) % result.shape[longest]] + place[longest + 1:]
    return result.at[tuple(place)].set(low).at[tuple(neighbour)].set(top_value)


def level_of(rng, dims, cuts, low, largest):
    gain, own = 1.0, jax.random.fold_in(rng, 6)
    for position, shards_of in cuts:
        steps = jnp.exp(jax.random.uniform(jax.random.fold_in(own, position), (shards_of,), jnp.float32, low / len(cuts), largest / len(cuts)))
        gain = gain * jnp.repeat(steps, dims[position] // shards_of).reshape([-1 if axis == position else 1 for axis in range(len(dims))])
    return gain


def split_up(count, total, limit, lean):
    portions = [(1 << 20) // math.isqrt(grade ** lean) + 1 for grade in range(2, count + 1)]
    rest, given = total - limit - (count - 1), [1] * (count - 1)
    while rest > 0:
        candidates = [i for i in range(count - 1) if given[i] < limit]
        whole, remaining = sum([portions[i] for i in candidates]), rest
        for i in candidates:
            extra = min(limit - given[i], max(1, remaining * portions[i] // whole), rest)
            given[i] = given[i] + extra
            rest = rest - extra
    return np.array([limit] + given)


def uneven_parts(own_key, count, total, reach, skew):
    if count == 2:
        one = jax.random.randint(own_key, (), max(1, total - reach), min(reach, total - 1) + 1)
        return jnp.stack([one, total - one])
    lengths = jnp.asarray(split_up(count, total, reach, skew), jnp.int32)
    twos = (count - 1) // 2
    giver, receiver = lengths[1:1 + 2 * twos:2], lengths[2:2 + 2 * twos:2]
    margin = jnp.minimum(giver - 1, reach - receiver)
    passed = jax.random.randint(jax.random.fold_in(own_key, 1), (twos,), 0, 1 << 20) % (margin + 1)
    lengths = lengths.at[1:1 + 2 * twos:2].set(giver - passed).at[2:2 + 2 * twos:2].set(receiver + passed)
    return lengths[jax.random.permutation(jax.random.fold_in(own_key, 2), count)]


def normal_values(stream_key, dims, width, bound, pieces=(), kind=jnp.bfloat16):
    entries = jax.random.normal(stream_key, dims, jnp.float32) * width
    if len(pieces) > 0:
        entries = level_of(stream_key, dims, pieces, -0.22, 0.18) * entries
    return jnp.clip(entries, min=-bound, max=bound).astype(kind)


def setup_inputs(seed: int = 0) -> dict:
    keys = jax.random.split(jax.random.key(seed), 8)
    roll_query = draw_roll_query(jax.random.fold_in(keys[7], 71), 0)
    roll_keys = draw_roll_keys(jax.random.fold_in(keys[7], 71), 0)
    roll_values = normal_values(keys[2], (SEQS, SEQ_LEN, HK * HD), 1.0, 6.0, ((0, 16), (1, 16)))
    pack_dest = draw_pack_dest(jax.random.fold_in(keys[7], 71), 0)
    segment_ids = jax.vmap(lambda own: jnp.searchsorted(jnp.cumsum(uneven_parts(own, SEGS, SEQ_LEN, SEQ_LEN // 2, 2)), jnp.arange(SEQ_LEN), side="right"))(jax.random.split(keys[4], SEQS)).reshape((SEQS, SEQ_LEN)).astype(jnp.int32)
    reward_bins = with_ends(jax.random.randint(keys[5], (SEQS, SEGS), 0, BINS), jax.random.fold_in(keys[5], 1), 0, BINS - 1).astype(jnp.int32)
    reward_weight = normal_values(keys[6], (HQ * HD,), HD ** -0.5, 0.5, (), jnp.float32)
    return dict(roll_query=roll_query, roll_keys=roll_keys, roll_values=roll_values, pack_dest=pack_dest, segment_ids=segment_ids, reward_bins=reward_bins, reward_weight=reward_weight)


NEG = -1e+30

def attend_sequence(query_rows, key_rows, value_rows, segments):
    seq_total = query_rows.shape[0]
    group_size = HQ // HK
    score_scale = 1.0 / math.sqrt(HD)
    positions = jnp.arange(seq_total, dtype=jnp.int32)
    allowed = (segments[:, None] == segments[None, :]) & (positions[None, :] <= positions[:, None])
    query_heads = query_rows.reshape(seq_total, HK, group_size, HD)
    key_heads = key_rows.reshape(seq_total, HK, HD)
    value_heads = value_rows.reshape(seq_total, HK, HD)

    def one_group(head_index):
        queries = jnp.take(query_heads, head_index, axis=1).astype(jnp.float32)
        keys_one = jnp.take(key_heads, head_index, axis=1).astype(jnp.float32)
        values_one = jnp.take(value_heads, head_index, axis=1).astype(jnp.float32)
        scores = jnp.einsum('qjd,kd->jqk', queries, keys_one, precision=lax.Precision.HIGHEST) * score_scale
        scores = jnp.where(allowed[None], scores, NEG)
        row_top = lax.optimization_barrier(jnp.max(scores, axis=-1))
        weights = jnp.where(allowed[None], jnp.exp(scores - row_top[..., None]), 0.0)
        row_total = lax.optimization_barrier(jnp.sum(weights, axis=-1))
        rounded = lax.optimization_barrier(weights.astype(jnp.bfloat16)).astype(jnp.float32)
        mixed_rows = jnp.einsum('jqk,kd->qjd', rounded, values_one, precision=lax.Precision.HIGHEST)
        return mixed_rows / jnp.transpose(row_total)[..., None]
    per_group = lax.map(one_group, jnp.arange(HK, dtype=jnp.int32))
    return jnp.transpose(per_group, (1, 0, 2, 3)).reshape(seq_total, HQ * HD).astype(jnp.bfloat16)

def reference(roll_query, roll_keys, roll_values, pack_dest, segment_ids, reward_bins, reward_weight):
    column_count = pack_dest.shape[1]
    seq_total = roll_query.shape[1]
    source_ids = jnp.arange(SEQS, dtype=jnp.int32)
    matches = pack_dest[:, None, :] == source_ids[None, :, None]
    source_of = lax.optimization_barrier(jnp.sum(jnp.where(matches, source_ids[:, None, None], 0), axis=0)).astype(jnp.int32)
    columns = jnp.arange(column_count, dtype=jnp.int32)
    query_blocks = roll_query.reshape(SEQS, column_count, BLK, HQ * HD)
    key_blocks = roll_keys.reshape(SEQS, column_count, BLK, HK * HD)
    value_blocks = roll_values.reshape(SEQS, column_count, BLK, HK * HD)

    def one_sequence(seq_index):
        sources = source_of[seq_index]
        packed_query = query_blocks[sources, columns].reshape(seq_total, HQ * HD)
        packed_keys = key_blocks[sources, columns].reshape(seq_total, HK * HD)
        packed_values = value_blocks[sources, columns].reshape(seq_total, HK * HD)
        segments = segment_ids[seq_index]
        attended = attend_sequence(packed_query, packed_keys, packed_values, segments)
        next_seg = jnp.concatenate([segments[1:], jnp.full((1,), -1, jnp.int32)])
        is_end = segments != next_seg
        row_reward = jnp.dot(attended.astype(jnp.float32), reward_weight, precision=lax.Precision.HIGHEST)
        kept = jnp.where(is_end, row_reward, 0.0)
        bin_of = reward_bins[seq_index][segments].astype(jnp.int32)
        local_hist = jnp.zeros((BINS,), jnp.float32).at[bin_of].add(kept)
        return (attended, local_hist)
    attended_all, hist_rows = lax.map(one_sequence, jnp.arange(SEQS, dtype=jnp.int32))
    return (attended_all, lax.optimization_barrier(jnp.sum(hist_rows, axis=0)))
```

```python
import functools
import math

import jax
import jax.numpy as jnp
from jax import lax
from jax.experimental import pallas as pl
from jax.experimental.pallas import tpu as pltpu
from jax.sharding import PartitionSpec as P

HQ = 32
HK = 4
HD = 128
TQ = 128
BLK = 8
NB = 16
SEGS = 16
BINS = 512
GROUP = HQ // HK
WIN = 9
NEG = -1e30
SCALE = math.log2(math.e) / math.sqrt(HD)
MESH = pl.DeviceIdType.MESH

ROUTES = (
    (264, 7, 1, 263, 8, 257, -2, 24, 23, -18, 279, -23, 360, -6, 88, -3, 39, -22, 344),
    (16, 274, 281, 18, 25, -1, 272, 2, -17, -20, 258, 313, -3, 32),
    (42, 291, 298, 35, -18, -20, 305, 275, -2, 33, 19, -1, 3, -17, 259),
    (315, 52, 306, 308, 59, -21, -19, 331, 292, -3, 36, -18, 276, -2, 20, -1, -17),
    (323, 76, 69, 332, 325, -4, 53, -20, -23, 364, 309, -19, 293, -3, 37, -18, -1, -2, -17),
    (86, 349, 93, 342, -23, -5, 356, 70, 365, -21, -24, 326, 381, -4, 54, -1, -20, 4, 310, -19, -17, 260, 294, -3, -2, 38, -18),
    (357, 110, 359, 103, 366, -24, -6, 373, 382, 87, -22, -1, 5, 343, -5, -17, 261, 71, -21, -2, 21, 327, -4, -18, 55, 277, -20, 311, -19, 295, -3),
    (374, 127, 383, -1, -23, 6, 352, -17, -7, 262, 111, -6, -2, 22, 80, -22, -18, 278, 336, -5, 79, -21, -4, -3, -20, -19),
    (399, 393, 143, 137, -10, -17, 159, -26, -1, 415, -18, -8, 121, -2, -24, -11, 175, 377, -23, -3, 361, -7, -20, 105, -6, -19, 89, -22, -4, -5, -21),
    (154, 152, 410, 408, -25, -18, -11, 280, 394, -9, -2, 138, 168, -3, 40, -19, -20, -8, 312, 122, -24, 378, 296, -4, -23, 56, 362, -21, -7, 328, -5, -6, -22),
    (427, 169, 171, -10, -3, 41, 155, -26, -19, 297, 411, -20, -25, 395, -9, -4, 57, 139, -21, 329, -5, -8, 123, 73, -24, -22, 345, -23, -7, -6),
    (188, 444, -27, -20, 314, 428, -11, -4, 172, 58, -10, -5, -21, 330, 156, -26, -22, 412, 74, -25, -6, 346, 396, -9, -7, 140, 106, -23, -8, 90, -24),
    (205, 461, -12, -5, 189, 75, -28, -21, 445, -22, -27, 347, 429, -11, -6, 91, -23, 173, -7, -10, 107, -26, -24, 363, -8, -25, 379, -9),
    (222, 478, -13, -22, 206, 348, -29, -6, 462, 92, -7, -12, -23, 190, 108, -28, -25, -24, 380, 446, -8, -27, 124, 430, -10, -11, -26, -9),
    (239, 495, -14, -7, 223, 109, -30, -23, -25, 479, 397, -13, -24, -8, 125, 207, -29, -10, 157, 463, -12, -26, 191, 413, -28, -9, 141, 447, -27, -11, 431),
    (-25, -15, 398, -8, 120, -31, -9, 126, -24, 376, -14, -10, 158, -30, -26, 414, -7, 104, -13, 142, -11, -29, 174, -5, -12, 72, -28, -27),
)


def remote(src, dst, send_sem, recv_sem, device_id):
    return pltpu.make_async_remote_copy(
        src_ref=src, dst_ref=dst, send_sem=send_sem, recv_sem=recv_sem, device_id=device_id, device_id_type=MESH
    )


def kernel(
    dest_ref, bins_ref, rq_ref, rk_ref, rv_ref, seg_ref, rw_ref,
    out_ref, hist_ref,
    qsend, qrecv, kvsend, kvrecv, qs, kv, segbuf, bias, racc, hist_a, hist_b,
    q_ss, q_rs, kv_ss, kv_rs, seg_ss, seg_rs, item_ss, item_rs, ha_ss, ha_rs, hb_ss, hb_rs,
):
    dp = lax.axis_index("dp")
    ctx = lax.axis_index("ctx")

    for b in range(1, WIN):
        @pl.when(b > ctx)
        def _():
            for h in range(2):
                kv[h, b] = jnp.zeros((HK, TQ, HD), jnp.bfloat16)

    barrier = pltpu.get_barrier_semaphore()

    def greet(k, carry):
        pl.semaphore_signal(barrier, inc=1, device_id={"dp": (dp + k) % 16}, device_id_type=MESH)
        pl.semaphore_signal(barrier, inc=1, device_id={"ctx": (ctx + k) % 16}, device_id_type=MESH)
        return carry

    lax.fori_loop(1, 16, greet, 0)

    def fill_kv(d, carry):
        inv = jnp.int32(0)
        for j in range(NB):
            inv = jnp.where(dest_ref[dp, j] == d, j, inv)
        kvsend[d, :, : HK * HD] = rk_ref[inv]
        kvsend[d, :, HK * HD :] = rv_ref[inv]
        return carry

    lax.fori_loop(0, NB, fill_kv, 0)
    pl.semaphore_wait(barrier, 30)

    def kv_copy(k):
        d = (dp + k) % 16
        return remote(kvsend.at[d], kvrecv.at[dp], kv_ss.at[k], kv_rs.at[dp], {"dp": d})

    def kv_start(k, carry):
        kv_copy(k).start()
        return carry

    lax.fori_loop(1, 16, kv_start, 0)
    kvrecv[dp] = kvsend[dp]
    segbuf[ctx] = seg_ref[0]

    def seg_copy(k):
        return remote(seg_ref.at[0], segbuf.at[ctx], seg_ss.at[k], seg_rs.at[ctx], {"ctx": (ctx + k) % 16})

    def seg_start(k, carry):
        seg_copy(k).start()
        return carry

    def fill_q(d, carry):
        inv = jnp.int32(0)
        for j in range(NB):
            inv = jnp.where(dest_ref[dp, j] == d, j, inv)
        qsend[d] = rq_ref[inv]
        return carry

    lax.fori_loop(0, NB, fill_q, 0)

    def q_copy(k):
        d = (dp + k) % 16
        return remote(qsend.at[d], qrecv.at[dp], q_ss.at[k], q_rs.at[dp], {"dp": d})

    def q_start(k, carry):
        q_copy(k).start()
        return carry

    def kv_wait(k, carry):
        s = (dp + k) % 16
        remote(kvsend.at[s], kvrecv.at[s], kv_ss.at[k], kv_rs.at[s], {"dp": s}).wait_recv()
        return carry

    lax.fori_loop(1, 16, kv_wait, 0)

    def source_of(j):
        src = jnp.int32(0)
        for s in range(16):
            src = jnp.where(dest_ref[s, j] == dp, s, src)
        return src

    def pack_kv(jj, carry):
        top = kvrecv[source_of(2 * jj)].astype(jnp.float32)
        low = kvrecv[source_of(2 * jj + 1)].astype(jnp.float32)
        rows = jnp.concatenate([top, low], axis=0).astype(jnp.bfloat16)
        at = pl.ds(pl.multiple_of(jj * 16, 16), 16)
        for h in range(2):
            for g in range(HK):
                lane = (h * HK + g) * HD
                kv[h, ctx, g, at, :] = rows[:, lane : lane + HD]
        return carry

    lax.fori_loop(0, NB // 2, pack_kv, 0)

    def item_copy(h, b, to, slot):
        return remote(kv.at[h, b], kv.at[h, b], item_ss.at[slot], item_rs.at[h * 16 + b], {"ctx": to})

    def run_steps(steps, slot):
        for n in steps:
            if n < 0:
                item = -1 - n
                item_copy(item // 16, item % 16, ctx, 0).wait_recv()
            else:
                item = n // 16
                item_copy(item // 16, item % 16, n % 16, slot).start()
                slot += 1
        return slot

    first = [next((i for i, n in enumerate(steps) if n < 0), len(steps)) for steps in ROUTES]
    for c, steps in enumerate(ROUTES):
        @pl.when(ctx == c)
        def _():
            run_steps(steps[: first[c]], 0)

    lax.fori_loop(1, 16, q_start, 0)
    qrecv[dp] = qsend[dp]
    lax.fori_loop(1, 16, seg_start, 0)
    for c, steps in enumerate(ROUTES):
        @pl.when(ctx == c)
        def _():
            run_steps(steps[first[c] :], first[c])

    def q_wait(k, carry):
        s = (dp + k) % 16
        remote(qsend.at[s], qrecv.at[s], q_ss.at[k], q_rs.at[s], {"dp": s}).wait_recv()
        return carry

    lax.fori_loop(1, 16, q_wait, 0)

    def pack_q(jj, carry):
        top = qrecv[source_of(2 * jj)].astype(jnp.float32)
        low = qrecv[source_of(2 * jj + 1)].astype(jnp.float32)
        rows = jnp.concatenate([top, low], axis=0).astype(jnp.bfloat16)
        at = pl.ds(pl.multiple_of(jj * 16, 16), 16)
        for h in range(HQ):
            qs[h, at, :] = rows[:, h * HD : (h + 1) * HD]
        return carry

    lax.fori_loop(0, NB // 2, pack_q, 0)

    def seg_wait(k, carry):
        s = (ctx + k) % 16
        remote(seg_ref.at[0], segbuf.at[s], seg_ss.at[k], seg_rs.at[s], {"ctx": s}).wait_recv()
        return carry

    lax.fori_loop(1, 16, seg_wait, 0)

    def column(row):
        return jnp.transpose(jnp.broadcast_to(row.astype(jnp.float32), (TQ, TQ)))

    lane = lax.broadcasted_iota(jnp.int32, (TQ, TQ), 1)
    sub = lax.broadcasted_iota(jnp.int32, (TQ, TQ), 0)
    seg_row = seg_ref[0]
    seg_col = column(seg_row)
    base = jnp.maximum(ctx - (WIN - 1), 0)
    for w in range(WIN):
        keys = segbuf[base + w].astype(jnp.float32)
        allowed = (seg_col == keys) & ((base + w - ctx) * TQ + lane <= sub)
        bias[:, w * TQ : (w + 1) * TQ] = jnp.where(allowed, 0.0, NEG)

    racc[...] = jnp.zeros_like(racc)

    def heads(i, carry):
        per = 2
        g = i // (GROUP // per)
        q = qs[pl.ds(i * per, per)].reshape(per * TQ, HD)
        k = kv[0, pl.ds(base, WIN), g].reshape(WIN * TQ, HD)
        v = kv[1, pl.ds(base, WIN), g].reshape(WIN * TQ, HD)
        s = lax.dot_general(q, k, (((1,), (1,)), ((), ())), preferred_element_type=jnp.float32)
        s = (s * SCALE).reshape(per, TQ, WIN * TQ) + bias[...][None]
        top = jnp.max(s, axis=-1, keepdims=True)
        p = jnp.exp2(s - top)
        total = jnp.sum(p, axis=-1, keepdims=True)
        pb = p.astype(jnp.bfloat16).reshape(per * TQ, WIN * TQ)
        o = jnp.dot(pb, v, preferred_element_type=jnp.float32).reshape(per, TQ, HD)
        o = (o / total).astype(jnp.bfloat16)
        for e in range(per):
            at = pl.ds(pl.multiple_of((i * per + e) * HD, HD), HD)
            out_ref[:, at] = o[e]
            racc[...] += o[e].astype(jnp.float32) * rw_ref[:, at]
        return carry

    lax.fori_loop(0, HQ // 2, heads, 0)

    lane_row = lane[:1]
    following = jnp.where(
        lane_row == TQ - 1, pltpu.roll(segbuf[(ctx + 1) % 16], TQ - 1, 1), pltpu.roll(seg_row, TQ - 1, 1)
    )
    last = (lane_row == TQ - 1) & (ctx == 15)
    is_end = jnp.where((following != seg_row) | last, 1.0, 0.0)
    bin_row = jnp.zeros((1, TQ), jnp.int32)
    for s in range(SEGS):
        bin_row = jnp.where(seg_row == s, bins_ref[0, s], bin_row)
    end_col = column(is_end)
    bin_col = column(bin_row)
    reward = jnp.sum(racc[...], axis=1, keepdims=True)
    kept = jnp.where(end_col > 0.5, reward, 0.0)
    parts = []
    for k in range(BINS // TQ):
        hit = bin_col == (lane + k * TQ).astype(jnp.float32)
        parts.append(jnp.sum(jnp.where(hit, kept, 0.0), axis=0, keepdims=True))
    hist_a[dp] = jnp.concatenate(parts, axis=1)

    def hist_copy(buf, ss, rs, axis, me, k):
        return remote(buf.at[me], buf.at[me], ss.at[k], rs.at[me], {axis: (me + k) % 16})

    def hist_round(buf, ss, rs, axis, me):
        def start(k, carry):
            hist_copy(buf, ss, rs, axis, me, k).start()
            return carry

        def wait(k, carry):
            s = (me + k) % 16
            remote(buf.at[s], buf.at[s], ss.at[k], rs.at[s], {axis: s}).wait_recv()
            return carry

        lax.fori_loop(1, 16, start, 0)
        lax.fori_loop(1, 16, wait, 0)
        return jnp.sum(buf[...], axis=0)

    hist_b[ctx] = hist_round(hist_a, ha_ss, ha_rs, "dp", dp)
    hist_ref[...] = hist_round(hist_b, hb_ss, hb_rs, "ctx", ctx)

    def drain(k, carry):
        kv_copy(k).wait_send()
        q_copy(k).wait_send()
        seg_copy(k).wait_send()
        hist_copy(hist_a, ha_ss, ha_rs, "dp", dp, k).wait_send()
        hist_copy(hist_b, hb_ss, hb_rs, "ctx", ctx, k).wait_send()
        return carry

    lax.fori_loop(1, 16, drain, 0)
    sends = jnp.int32(0)
    for c, steps in enumerate(ROUTES):
        sends += jnp.where(ctx == c, sum(n >= 0 for n in steps), 0)

    def drain_items(slot, carry):
        item_copy(0, 0, ctx, slot).wait_send()
        return carry

    lax.fori_loop(0, sends, drain_items, 0)


def local(roll_query, roll_keys, roll_values, pack_dest, segment_ids, reward_bins, reward_weight):
    vmem = pl.BlockSpec(memory_space=pltpu.VMEM)
    smem = pl.BlockSpec(memory_space=pltpu.SMEM)
    bf16, f32, i32 = jnp.bfloat16, jnp.float32, jnp.int32
    dma = pltpu.SemaphoreType.DMA
    most = max(sum(n >= 0 for n in steps) for steps in ROUTES)
    out, hist = pl.pallas_call(
        kernel,
        out_shape=(jax.ShapeDtypeStruct((TQ, HQ * HD), bf16), jax.ShapeDtypeStruct((1, BINS), f32)),
        in_specs=[smem, smem, vmem, vmem, vmem, vmem, vmem],
        out_specs=(vmem, vmem),
        scratch_shapes=[
            pltpu.VMEM((16, BLK, HQ * HD), bf16),
            pltpu.VMEM((16, BLK, HQ * HD), bf16),
            pltpu.VMEM((16, BLK, 2 * HK * HD), bf16),
            pltpu.VMEM((16, BLK, 2 * HK * HD), bf16),
            pltpu.VMEM((HQ, TQ, HD), bf16),
            pltpu.VMEM((2, 16, HK, TQ, HD), bf16),
            pltpu.VMEM((16, 1, TQ), i32),
            pltpu.VMEM((TQ, WIN * TQ), f32),
            pltpu.VMEM((TQ, HD), f32),
            pltpu.VMEM((16, 1, BINS), f32),
            pltpu.VMEM((16, 1, BINS), f32),
            dma((16,)), dma((16,)), dma((16,)), dma((16,)), dma((16,)), dma((16,)),
            dma((most,)), dma((32,)), dma((16,)), dma((16,)), dma((16,)), dma((16,)),
        ],
        compiler_params=pltpu.CompilerParams(
            collective_id=0, has_side_effects=True, vmem_limit_bytes=48 * 1024 * 1024
        ),
    )(
        pack_dest,
        reward_bins,
        roll_query.reshape(NB, BLK, HQ * HD),
        roll_keys.reshape(NB, BLK, HK * HD),
        roll_values.reshape(NB, BLK, HK * HD),
        segment_ids.reshape(1, 1, TQ),
        reward_weight.reshape(1, HQ * HD),
    )
    return out.reshape(1, TQ, HQ * HD), hist.reshape(BINS)


def solution(mesh):
    in_specs = (
        P("dp", "ctx", None),
        P("dp", "ctx", None),
        P("dp", "ctx", None),
        P(None, "ctx"),
        P("dp", "ctx"),
        P("dp", None),
        P(),
    )
    out_specs = (P("dp", "ctx", None), P())
    return jax.shard_map(local, mesh=mesh, in_specs=in_specs, out_specs=out_specs, check_vma=False)
```

```python
import functools
import math

import jax
import jax.numpy as jnp
from jax import lax
from jax.experimental import pallas as pl
from jax.experimental.pallas import tpu as pltpu
from jax.sharding import PartitionSpec as P

HQ = 32
HK = 4
HD = 128
TQ = 128
BLK = 8
NB = 16
SEGS = 16
BINS = 512
GROUP = HQ // HK
WIN = 9
PER = 2
HALF = 8
NEG = -1e30
SCALE = math.log2(math.e) / math.sqrt(HD)
MESH = pl.DeviceIdType.MESH

ROUTES = (
    (264, 7, 1, 263, 257, -18, 8, 279, -2, -7, 104, 23, -19, 295, -3, 24, -22, 39, 337, -20, 344, 311, 312),
    (272, 281, 18, 16, 274, -1, -19, 297, 288, 2, -17, -3, 32, 25, 258, -20, 304, 313, -22, 345),
    (35, 42, 289, 291, 33, -20, -2, 314, 19, 305, -18, -21, 275, 330, -1, 3, -6, -17, 90, 259, -7, 106),
    (306, 52, 59, 308, -21, -3, 322, 331, 36, -19, -6, 82, 292, 91, -2, 20, -7, -18, 98, 107, 276, -1, 315, -17),
    (323, 76, 325, 69, -4, -6, 83, 92, 53, -20, -7, 99, 108, 309, -3, 37, -19, -24, 380, 293, -2, -1, 332, -18, -17),
    (84, 349, 342, 86, -7, -21, 100, 109, 326, -5, -24, 372, 381, 70, -4, 54, -1, -20, 4, 93, 310, -17, -3, 260, 38, -18, -19, -2),
    (101, 366, 103, 359, -24, -22, 373, 382, 343, -6, -1, 5, 110, 87, -21, -17, 261, 327, -5, -18, 277, 71, -4, -2, 21, 55, -20, -19, -3),
    (374, 127, -1, -7, 6, 96, 383, -17, -23, 262, 367, -18, -22, 278, 336, -2, -6, 22, 95, -19, -21, 294, -3, -5, -20, -4),
    (393, 143, 137, 399, -10, 159, -17, -26, 415, -11, -1, -8, 121, 175, -18, -7, -24, -19, 377, -3, 105, -2, -23, -4, 361, -22, -6, -21, -5, -20),
    (410, 152, 154, 408, -25, -11, 394, 168, -18, -9, 138, 280, -19, -3, 298, 296, 40, -2, -8, -4, 122, 56, -20, -24, -21, 378, 328, -7, -5, 72, -22, -23, -6),
    (169, 427, 171, -26, 411, -3, -10, 41, 155, -25, -20, -4, 57, 395, -9, 139, -21, -19, -5, 329, 73, -6, -8, -22, 123, 89, -7, -24, -23),
    (444, 188, -27, 428, -4, -11, 58, 172, -26, -21, -5, 412, 74, -10, 156, -6, -22, -25, 346, 396, -9, -7, -23, 362, -20, -24, -8),
    (205, 461, -28, 445, -5, -12, 75, 189, -27, -6, -22, 347, 429, -11, 173, -7, -23, -26, 363, 413, -9, -10, -24, 379, -8, -25, -21),
    (222, 478, -13, 206, -22, -29, 348, 462, -28, -7, -23, 446, 364, -12, -9, 190, 140, -24, -27, -8, 430, 124, -11, -6, -10, -26, -25),
    (239, 495, -14, 223, -23, -30, 365, -9, 479, -13, 141, -24, -8, 207, -29, 125, -10, 463, -7, -28, 157, -25, 447, -12, 397, -11, 191, -27, -26, 431),
    (-9, -15, 142, -8, -25, -31, 120, 126, -10, -14, 158, -24, 376, -26, -30, 398, -23, -11, -13, 360, 174, -29, 414, -6, 88, -28, -12, -27),
)
CUTS = (22, 20, 22, 24, 25, 28, 29, 26, 24, 27, 25, 24, 26, 26, 28, 26)


def remote(src, dst, send_sem, recv_sem, device_id):
    return pltpu.make_async_remote_copy(
        src_ref=src, dst_ref=dst, send_sem=send_sem, recv_sem=recv_sem, device_id=device_id, device_id_type=MESH
    )


def kernel(
    dest_ref, bins_ref, rq_hbm, rk_hbm, rv_hbm, seg_ref, rw_hbm,
    out_ref, hist_ref,
    rq_ref, rk_ref, rv_ref, rw_ref, qsend, qrecv, kvsend, kvrecv, qs, qe, kv, segbuf, bias, bias_end, hist_a, hist_b,
    in_sem, q_ss, q_rs, kv_ss, kv_rs, seg_ss, seg_rs, item_ss, item_rs, ha_ss, ha_rs, hb_ss, hb_rs,
):
    dp = lax.axis_index("dp")
    ctx = lax.axis_index("ctx")
    loads = [
        pltpu.make_async_copy(src, dst, in_sem.at[i])
        for i, (src, dst) in enumerate(
            ((rk_hbm, rk_ref), (rv_hbm, rv_ref), (rq_hbm, rq_ref), (rw_hbm, rw_ref))
        )
    ]
    for load in loads:
        load.start()

    barrier = pltpu.get_barrier_semaphore()

    def greet(k, carry):
        pl.semaphore_signal(barrier, inc=1, device_id={"dp": (dp + k) % 16}, device_id_type=MESH)
        pl.semaphore_signal(barrier, inc=1, device_id={"ctx": (ctx + k) % 16}, device_id_type=MESH)
        return carry

    lax.fori_loop(1, 16, greet, 0)

    def fill_kv(d, carry):
        inv = jnp.int32(0)
        for j in range(NB):
            inv = jnp.where(dest_ref[dp, j] == d, j, inv)
        kvsend[d, :, : HK * HD] = rk_ref[inv]
        kvsend[d, :, HK * HD :] = rv_ref[inv]
        return carry

    loads[0].wait()
    loads[1].wait()
    lax.fori_loop(0, NB, fill_kv, 0)
    pl.semaphore_wait(barrier, 30)

    def kv_copy(k):
        d = (dp + k) % 16
        return remote(kvsend.at[d], kvrecv.at[dp], kv_ss.at[k], kv_rs.at[dp], {"dp": d})

    def kv_start(k, carry):
        kv_copy(k).start()
        return carry

    lax.fori_loop(1, 16, kv_start, 0)
    kvrecv[dp] = kvsend[dp]
    segbuf[ctx] = seg_ref[0]

    def seg_copy(k):
        return remote(seg_ref.at[0], segbuf.at[ctx], seg_ss.at[k], seg_rs.at[ctx], {"ctx": (ctx + k) % 16})

    def seg_start(k, carry):
        seg_copy(k).start()
        return carry

    def fill_q(d, carry):
        inv = jnp.int32(0)
        for j in range(NB):
            inv = jnp.where(dest_ref[dp, j] == d, j, inv)
        qsend[d] = rq_ref[inv]
        return carry

    loads[2].wait()
    lax.fori_loop(0, NB, fill_q, 0)
    loads[3].wait()

    def q_copy(k):
        d = (dp + k) % 16
        return remote(qsend.at[d], qrecv.at[dp], q_ss.at[k], q_rs.at[dp], {"dp": d})

    def q_start(k, carry):
        q_copy(k).start()
        return carry

    def kv_wait(k, carry):
        s = (dp + k) % 16
        remote(kvsend.at[s], kvrecv.at[s], kv_ss.at[k], kv_rs.at[s], {"dp": s}).wait_recv()
        return carry

    lax.fori_loop(1, 16, kv_wait, 0)

    def source_of(j):
        src = jnp.int32(0)
        for s in range(16):
            src = jnp.where(dest_ref[s, j] == dp, s, src)
        return src

    def pack_kv(jj, carry):
        top = kvrecv[source_of(2 * jj)].astype(jnp.float32)
        low = kvrecv[source_of(2 * jj + 1)].astype(jnp.float32)
        rows = jnp.concatenate([top, low], axis=0).astype(jnp.bfloat16)
        at = pl.ds(pl.multiple_of(jj * 16, 16), 16)
        for h in range(2):
            for g in range(HK):
                lane = (h * HK + g) * HD
                kv[h, ctx, g, at, :] = rows[:, lane : lane + HD]
        return carry

    lax.fori_loop(0, NB // 2, pack_kv, 0)

    def item_copy(h, b, to, slot):
        return remote(kv.at[h, b], kv.at[h, b], item_ss.at[slot], item_rs.at[h * 16 + b], {"ctx": to})

    def run_steps(steps, slot):
        for n in steps:
            if n < 0:
                item = -1 - n
                item_copy(item // 16, item % 16, ctx, 0).wait_recv()
            else:
                item = n // 16
                item_copy(item // 16, item % 16, n % 16, slot).start()
                slot += 1
        return slot

    first = [next((i for i, n in enumerate(steps) if n < 0), len(steps)) for steps in ROUTES]
    sent = [sum(n >= 0 for n in steps[:cut]) for steps, cut in zip(ROUTES, CUTS)]
    for c, steps in enumerate(ROUTES):
        @pl.when(ctx == c)
        def _():
            run_steps(steps[: first[c]], 0)

    lax.fori_loop(1, 16, q_start, 0)
    qrecv[dp] = qsend[dp]
    lax.fori_loop(1, 16, seg_start, 0)
    for c, steps in enumerate(ROUTES):
        @pl.when(ctx == c)
        def _():
            for h in range(2):
                for b in range(c + 1, WIN):
                    if -1 - (h * 16 + b) not in steps:
                        kv[h, b] = jnp.zeros((HK, TQ, HD), jnp.bfloat16)
            run_steps(steps[first[c] : CUTS[c]], first[c])

    def q_wait(k, carry):
        s = (dp + k) % 16
        remote(qsend.at[s], qrecv.at[s], q_ss.at[k], q_rs.at[s], {"dp": s}).wait_recv()
        return carry

    lax.fori_loop(1, 16, q_wait, 0)

    def pack_q(jj, carry):
        top = qrecv[source_of(2 * jj)].astype(jnp.float32)
        low = qrecv[source_of(2 * jj + 1)].astype(jnp.float32)
        rows = jnp.concatenate([top, low], axis=0).astype(jnp.bfloat16)
        at = pl.ds(pl.multiple_of(jj * 16, 16), 16)
        for h in range(HQ):
            qs[h, at, :] = rows[:, h * HD : (h + 1) * HD]
        return carry

    lax.fori_loop(0, NB // 2, pack_q, 0)

    def seg_wait(k, carry):
        s = (ctx + k) % 16
        remote(seg_ref.at[0], segbuf.at[s], seg_ss.at[k], seg_rs.at[s], {"ctx": s}).wait_recv()
        return carry

    lax.fori_loop(1, 16, seg_wait, 0)

    def column(row):
        return jnp.transpose(jnp.broadcast_to(row.astype(jnp.float32), (TQ, TQ)))

    lane = lax.broadcasted_iota(jnp.int32, (TQ, TQ), 1)
    sub = lax.broadcasted_iota(jnp.int32, (TQ, TQ), 0)
    seg_row = seg_ref[0]
    seg_col = column(seg_row)
    base = jnp.maximum(ctx - (WIN - 1), 0)
    for w in range(WIN):
        keys = segbuf[base + w].astype(jnp.float32)
        allowed = (seg_col == keys) & ((base + w - ctx) * TQ + lane <= sub)
        bias[:, w * TQ : (w + 1) * TQ] = jnp.where(allowed, 0.0, NEG)

    wide = (SEGS, TQ)
    lane_row = lane[:1]
    end_lane = lax.broadcasted_iota(jnp.int32, wide, 1).astype(jnp.float32)
    end_seg = lax.broadcasted_iota(jnp.int32, wide, 0)
    following = jnp.where(
        lane_row == TQ - 1, pltpu.roll(segbuf[(ctx + 1) % 16], TQ - 1, 1), pltpu.roll(seg_row, TQ - 1, 1)
    )
    is_end = (following != seg_row) | ((lane_row == TQ - 1) & (ctx == 15))
    pick = jnp.where((seg_row == end_seg) & is_end, 1.0, 0.0)
    end_pos = jnp.sum(pick * end_lane, axis=1, keepdims=True)
    has_end = jnp.sum(pick, axis=1, keepdims=True)
    pick = pick.astype(jnp.bfloat16)
    for w in range(WIN):
        offset = ((base + w - ctx) * TQ).astype(jnp.float32)
        allowed = (segbuf[base + w] == end_seg) & (end_lane + offset <= end_pos)
        bias_end[:, w * TQ : (w + 1) * TQ] = jnp.where(allowed, 0.0, NEG)
    for h in range(HQ):
        rows = jnp.dot(pick, qs[h], preferred_element_type=jnp.float32).astype(jnp.bfloat16)
        qe[h // GROUP, (h % GROUP) * SEGS : (h % GROUP + 1) * SEGS] = rows

    for c, steps in enumerate(ROUTES):
        @pl.when(ctx == c)
        def _():
            run_steps(steps[CUTS[c] :], sent[c])

    def attend(q, g, mask, per, rows):
        k = kv[0, pl.ds(base, WIN), g].reshape(WIN * TQ, HD)
        v = kv[1, pl.ds(base, WIN), g].reshape(WIN * TQ, HD)
        s = lax.dot_general(q, k, (((1,), (1,)), ((), ())), preferred_element_type=jnp.float32)
        s = (s * SCALE).reshape(per, rows, WIN * TQ) + mask[None]
        top = jnp.max(s, axis=-1, keepdims=True)
        p = jnp.exp2(s - top)
        total = jnp.sum(p, axis=-1, keepdims=True)
        pb = p.astype(jnp.bfloat16).reshape(per * rows, WIN * TQ)
        o = jnp.dot(pb, v, preferred_element_type=jnp.float32).reshape(per, rows, HD)
        return (o / total).astype(jnp.bfloat16)

    terms = jnp.zeros((SEGS, HD), jnp.float32)
    for g in range(HK):
        o = attend(qe[g], g, bias_end[...], GROUP, SEGS)
        for j in range(GROUP):
            h = g * GROUP + j
            terms += o[j].astype(jnp.float32) * rw_ref[h : h + 1, :]
    reward = jnp.where(has_end > 0.5, jnp.sum(terms, axis=1, keepdims=True), 0.0)
    bin_seg = lax.broadcasted_iota(jnp.int32, (SEGS, BINS), 0)
    bin_lane = lax.broadcasted_iota(jnp.int32, (SEGS, BINS), 1)
    bin_of = jnp.zeros((SEGS, BINS), jnp.int32)
    for s in range(SEGS):
        bin_of = jnp.where(bin_seg == s, bins_ref[0, s], bin_of)
    hist_a[dp] = jnp.sum(jnp.where(bin_of == bin_lane, reward, 0.0), axis=0, keepdims=True)

    def heads(i, carry):
        per = PER
        o = attend(qs[pl.ds(i * per, per)].reshape(per * TQ, HD), i // (GROUP // per), bias[...], per, TQ)
        for e in range(per):
            at = pl.ds(pl.multiple_of((i * per + e) * HD, HD), HD)
            out_ref[:, at] = o[e]
        return carry

    def hist_copy(buf, ss, rs, axis, me, k):
        return remote(buf.at[me], buf.at[me], ss.at[k], rs.at[me], {axis: (me + k) % 16})

    def hist_start(buf, ss, rs, axis, me):
        def start(k, carry):
            hist_copy(buf, ss, rs, axis, me, k).start()
            return carry

        lax.fori_loop(1, 16, start, 0)

    def hist_total(buf, ss, rs, axis, me):
        def wait(k, carry):
            s = (me + k) % 16
            remote(buf.at[s], buf.at[s], ss.at[k], rs.at[s], {axis: s}).wait_recv()
            return carry

        lax.fori_loop(1, 16, wait, 0)
        return jnp.sum(buf[...], axis=0)

    hist_start(hist_a, ha_ss, ha_rs, "dp", dp)
    lax.fori_loop(0, HALF, heads, 0)
    hist_b[ctx] = hist_total(hist_a, ha_ss, ha_rs, "dp", dp)
    hist_start(hist_b, hb_ss, hb_rs, "ctx", ctx)
    lax.fori_loop(HALF, HQ // PER, heads, 0)
    hist_ref[...] = hist_total(hist_b, hb_ss, hb_rs, "ctx", ctx)

    def drain(k, carry):
        kv_copy(k).wait_send()
        q_copy(k).wait_send()
        seg_copy(k).wait_send()
        hist_copy(hist_a, ha_ss, ha_rs, "dp", dp, k).wait_send()
        hist_copy(hist_b, hb_ss, hb_rs, "ctx", ctx, k).wait_send()
        return carry

    lax.fori_loop(1, 16, drain, 0)
    sends = jnp.int32(0)
    for c, steps in enumerate(ROUTES):
        sends += jnp.where(ctx == c, sum(n >= 0 for n in steps), 0)

    def drain_items(slot, carry):
        item_copy(0, 0, ctx, slot).wait_send()
        return carry

    lax.fori_loop(0, sends, drain_items, 0)


def local(roll_query, roll_keys, roll_values, pack_dest, segment_ids, reward_bins, reward_weight):
    vmem = pl.BlockSpec(memory_space=pltpu.VMEM)
    smem = pl.BlockSpec(memory_space=pltpu.SMEM)
    hbm = pl.BlockSpec(memory_space=pltpu.HBM)
    bf16, f32, i32 = jnp.bfloat16, jnp.float32, jnp.int32
    dma = pltpu.SemaphoreType.DMA
    most = max(sum(n >= 0 for n in steps) for steps in ROUTES)
    out, hist = pl.pallas_call(
        kernel,
        out_shape=(jax.ShapeDtypeStruct((TQ, HQ * HD), bf16), jax.ShapeDtypeStruct((1, BINS), f32)),
        in_specs=[smem, smem, hbm, hbm, hbm, vmem, hbm],
        out_specs=(vmem, vmem),
        scratch_shapes=[
            pltpu.VMEM((NB, BLK, HQ * HD), bf16),
            pltpu.VMEM((NB, BLK, HK * HD), bf16),
            pltpu.VMEM((NB, BLK, HK * HD), bf16),
            pltpu.VMEM((HQ, HD), f32),
            pltpu.VMEM((16, BLK, HQ * HD), bf16),
            pltpu.VMEM((16, BLK, HQ * HD), bf16),
            pltpu.VMEM((16, BLK, 2 * HK * HD), bf16),
            pltpu.VMEM((16, BLK, 2 * HK * HD), bf16),
            pltpu.VMEM((HQ, TQ, HD), bf16),
            pltpu.VMEM((HK, GROUP * SEGS, HD), bf16),
            pltpu.VMEM((2, 16, HK, TQ, HD), bf16),
            pltpu.VMEM((16, 1, TQ), i32),
            pltpu.VMEM((TQ, WIN * TQ), f32),
            pltpu.VMEM((SEGS, WIN * TQ), f32),
            pltpu.VMEM((16, 1, BINS), f32),
            pltpu.VMEM((16, 1, BINS), f32),
            dma((4,)), dma((16,)), dma((16,)), dma((16,)), dma((16,)), dma((16,)), dma((16,)),
            dma((most,)), dma((32,)), dma((16,)), dma((16,)), dma((16,)), dma((16,)),
        ],
        compiler_params=pltpu.CompilerParams(
            collective_id=0, has_side_effects=True, vmem_limit_bytes=60 * 1024 * 1024
        ),
    )(
        pack_dest,
        reward_bins,
        roll_query.reshape(NB, BLK, HQ * HD),
        roll_keys.reshape(NB, BLK, HK * HD),
        roll_values.reshape(NB, BLK, HK * HD),
        segment_ids.reshape(1, 1, TQ),
        reward_weight.reshape(HQ, HD),
    )
    return out.reshape(1, TQ, HQ * HD), hist.reshape(BINS)


def solution(mesh):
    in_specs = (
        P("dp", "ctx", None),
        P("dp", "ctx", None),
        P("dp", "ctx", None),
        P(None, "ctx"),
        P("dp", "ctx"),
        P("dp", None),
        P(),
    )
    out_specs = (P("dp", "ctx", None), P())
    return jax.shard_map(local, mesh=mesh, in_specs=in_specs, out_specs=out_specs, check_vma=False)
```

```python
import functools
import math

import jax
import jax.numpy as jnp
from jax import lax
from jax.experimental import pallas as pl
from jax.experimental.pallas import tpu as pltpu
from jax.sharding import PartitionSpec as P

HQ = 32
HK = 4
HD = 128
TQ = 128
BLK = 8
NB = 16
SEGS = 16
BINS = 512
GROUP = HQ // HK
WIN = 9
PER = 2
HALF = 8
NEG = -1e30
SCALE = math.log2(math.e) / math.sqrt(HD)
MESH = pl.DeviceIdType.MESH

ROUTES = (
    (264, 7, 1, 263, 257, -18, 8, 279, -2, -7, 104, 23, -19, 295, -3, 24, -22, 39, 337, -20, 344, 311, 312),
    (272, 281, 18, 16, 274, -1, -19, 297, 288, 2, -17, -3, 32, 25, 258, -20, 304, 313, -22, 345),
    (35, 42, 289, 291, 33, -20, -2, 314, 19, 305, -18, -21, 275, 330, -1, 3, -6, -17, 90, 259, -7, 106),
    (306, 52, 59, 308, -21, -3, 322, 331, 36, -19, -6, 82, 292, 91, -2, 20, -7, -18, 98, 107, 276, -1, 315, -17),
    (323, 76, 325, 69, -4, -6, 83, 92, 53, -20, -7, 99, 108, 309, -3, 37, -19, -24, 380, 293, -2, -1, 332, -18, -17),
    (84, 349, 342, 86, -7, -21, 100, 109, 326, -5, -24, 372, 381, 70, -4, 54, -1, -20, 4, 93, 310, -17, -3, 260, 38, -18, -19, -2),
    (101, 366, 103, 359, -24, -22, 373, 382, 343, -6, -1, 5, 110, 87, -21, -17, 261, 327, -5, -18, 277, 71, -4, -2, 21, 55, -20, -19, -3),
    (374, 127, -1, -7, 6, 96, 383, -17, -23, 262, 367, -18, -22, 278, 336, -2, -6, 22, 95, -19, -21, 294, -3, -5, -20, -4),
    (393, 143, 137, 399, -10, 159, -17, -26, 415, -11, -1, -8, 121, 175, -18, -7, -24, -19, 377, -3, 105, -2, -23, -4, 361, -22, -6, -21, -5, -20),
    (410, 152, 154, 408, -25, -11, 394, 168, -18, -9, 138, 280, -19, -3, 298, 296, 40, -2, -8, -4, 122, 56, -20, -24, -21, 378, 328, -7, -5, 72, -22, -23, -6),
    (169, 427, 171, -26, 411, -3, -10, 41, 155, -25, -20, -4, 57, 395, -9, 139, -21, -19, -5, 329, 73, -6, -8, -22, 123, 89, -7, -24, -23),
    (444, 188, -27, 428, -4, -11, 58, 172, -26, -21, -5, 412, 74, -10, 156, -6, -22, -25, 346, 396, -9, -7, -23, 362, -20, -24, -8),
    (205, 461, -28, 445, -5, -12, 75, 189, -27, -6, -22, 347, 429, -11, 173, -7, -23, -26, 363, 413, -9, -10, -24, 379, -8, -25, -21),
    (222, 478, -13, 206, -22, -29, 348, 462, -28, -7, -23, 446, 364, -12, -9, 190, 140, -24, -27, -8, 430, 124, -11, -6, -10, -26, -25),
    (239, 495, -14, 223, -23, -30, 365, -9, 479, -13, 141, -24, -8, 207, -29, 125, -10, 463, -7, -28, 157, -25, 447, -12, 397, -11, 191, -27, -26, 431),
    (-9, -15, 142, -8, -25, -31, 120, 126, -10, -14, 158, -24, 376, -26, -30, 398, -23, -11, -13, 360, 174, -29, 414, -6, 88, -28, -12, -27),
)
CUTS = (22, 20, 22, 24, 25, 28, 29, 26, 24, 27, 25, 24, 26, 26, 28, 26)


def remote(src, dst, send_sem, recv_sem, device_id):
    return pltpu.make_async_remote_copy(
        src_ref=src, dst_ref=dst, send_sem=send_sem, recv_sem=recv_sem, device_id=device_id, device_id_type=MESH
    )


def kernel(
    dest_ref, bins_ref, rq_hbm, rk_hbm, rv_hbm, seg_ref, rw_hbm,
    out_hbm, hist_ref,
    rq_ref, rk_ref, rv_ref, rw_ref, qsend, qrecv, ksend, krecv, vsend, vrecv, qs, qe, kbuf, vbuf, out_ref, seg_next,
    bias, bias_end, hist_a, hist_b,
    in_sem, out_sem, q_ss, q_rs, k_ss, k_rs, v_ss, v_rs, seg_ss, seg_rs, item_ss, item_rs,
    ha_ss, ha_rs, hb_ss, hb_rs, known,
):
    dp = lax.axis_index("dp")
    ctx = lax.axis_index("ctx")
    line = ctx // 8 * 8
    near = (line + (ctx + 1) % 8, line + (ctx + 7) % 8, (ctx + 8) % 16)
    loads = [
        pltpu.make_async_copy(src, dst, in_sem.at[i])
        for i, (src, dst) in enumerate(
            ((rk_hbm, rk_ref), (rv_hbm, rv_ref), (rq_hbm, rq_ref), (rw_hbm, rw_ref))
        )
    ]
    barrier = pltpu.get_barrier_semaphore()

    def greet(k, carry):
        pl.semaphore_signal(barrier, inc=1, device_id={"dp": (dp + k) % 16}, device_id_type=MESH)
        return carry

    lax.fori_loop(1, 16, greet, 0)
    for to in near:
        pl.semaphore_signal(barrier, inc=1, device_id={"ctx": to}, device_id_type=MESH)

    @pl.when(ctx == 7)
    def _():
        pl.semaphore_signal(barrier, inc=1, device_id={"ctx": 8}, device_id_type=MESH)

    for load in loads:
        load.start()

    def fill(src, dst):
        def body(d, carry):
            inv = jnp.int32(0)
            for j in range(NB):
                inv = jnp.where(dest_ref[dp, j] == d, j, inv)
            dst[d] = src[inv]
            return carry

        lax.fori_loop(0, NB, body, 0)

    def exchange(send, recv, ss, rs):
        def copy(k):
            d = (dp + k) % 16
            return remote(send.at[d], recv.at[dp], ss.at[k], rs.at[dp], {"dp": d})

        def start(k, carry):
            copy(k).start()
            return carry

        def wait(k, carry):
            s = (dp + k) % 16
            remote(send.at[s], recv.at[s], ss.at[k], rs.at[s], {"dp": s}).wait_recv()
            return carry

        return copy, start, wait

    k_copy, k_start, k_wait = exchange(ksend, krecv, k_ss, k_rs)
    v_copy, v_start, v_wait = exchange(vsend, vrecv, v_ss, v_rs)
    q_copy, q_start, q_wait = exchange(qsend, qrecv, q_ss, q_rs)
    loads[0].wait()
    fill(rk_ref, ksend)
    loads[1].wait()
    fill(rv_ref, vsend)
    pl.semaphore_wait(barrier, 18 + jnp.where(ctx == 8, 1, 0))
    lax.fori_loop(1, 16, k_start, 0)
    lax.fori_loop(1, 16, v_start, 0)
    krecv[dp] = ksend[dp]
    vrecv[dp] = vsend[dp]

    def spread(r):
        for to in near:
            pl.semaphore_signal(known.at[r], inc=1, device_id={"ctx": to}, device_id_type=MESH)

    def heard(r):
        pl.semaphore_wait(known.at[r], 3)

    seg_copy = remote(seg_ref.at[0], seg_next, seg_ss, seg_rs, {"ctx": (ctx + 15) % 16})
    spread(0)

    @pl.when(ctx > 0)
    def _():
        seg_copy.start()

    loads[2].wait()
    fill(rq_ref, qsend)
    loads[3].wait()
    heard(0)
    spread(1)

    def source_of(j):
        src = jnp.int32(0)
        for s in range(16):
            src = jnp.where(dest_ref[s, j] == dp, s, src)
        return src

    def rows_of(recv, jj):
        top = recv[source_of(2 * jj)].astype(jnp.float32)
        low = recv[source_of(2 * jj + 1)].astype(jnp.float32)
        return jnp.concatenate([top, low], axis=0).astype(jnp.bfloat16)

    def pack(recv, buf):
        def body(jj, carry):
            rows = rows_of(recv, jj)
            for g in range(HK):
                at = pl.ds(pl.multiple_of(g * TQ + jj * 16, 16), 16)
                buf[ctx, at, :] = rows[:, g * HD : (g + 1) * HD]
            return carry

        lax.fori_loop(0, NB // 2, body, 0)

    def item_copy(item, to, slot):
        buf = (kbuf, vbuf)[item // 16].at[item % 16]
        return remote(buf, buf, item_ss.at[slot], item_rs.at[item], {"ctx": to})

    slots = []
    for steps in ROUTES:
        k_sends = [n for n in steps if 0 <= n < 256]
        v_sends = [n for n in steps if n >= 256]
        slots.append({n: i for i, n in enumerate(k_sends + v_sends)})

    def run_steps(c, steps):
        for n in steps:
            if n < 0:
                item_copy(-1 - n, ctx, 0).wait_recv()
            else:
                item_copy(n // 16, n % 16, slots[c][n]).start()

    first = [next((i for i, n in enumerate(steps) if n < 0), len(steps)) for steps in ROUTES]
    seg_row = seg_ref[0]
    kbuf[ctx, HK * TQ :, :] = jnp.broadcast_to(seg_row.astype(jnp.float32), (16, TQ)).astype(jnp.bfloat16)
    lax.fori_loop(1, 16, k_wait, 0)
    pack(krecv, kbuf)
    for c, steps in enumerate(ROUTES):
        @pl.when(ctx == c)
        def _():
            run_steps(c, [n for n in steps[: first[c]] if n < 256])

    lax.fori_loop(1, 16, v_wait, 0)
    pack(vrecv, vbuf)
    for c, steps in enumerate(ROUTES):
        @pl.when(ctx == c)
        def _():
            run_steps(c, [n for n in steps[: first[c]] if n >= 256])

    lax.fori_loop(1, 16, q_start, 0)
    qrecv[dp] = qsend[dp]
    heard(1)
    spread(2)
    for c, steps in enumerate(ROUTES):
        @pl.when(ctx == c)
        def _():
            for b in range(c + 1, WIN):
                if -1 - b not in steps:
                    kbuf[b] = jnp.zeros((HK * TQ + 16, HD), jnp.bfloat16)
                if -1 - (16 + b) not in steps:
                    vbuf[b] = jnp.zeros((HK * TQ, HD), jnp.bfloat16)
            run_steps(c, steps[first[c] : CUTS[c]])

    heard(2)
    spread(3)
    lax.fori_loop(1, 16, q_wait, 0)

    def pack_q(jj, carry):
        rows = rows_of(qrecv, jj)
        at = pl.ds(pl.multiple_of(jj * 16, 16), 16)
        for h in range(HQ):
            qs[h, at, :] = rows[:, h * HD : (h + 1) * HD]
        return carry

    lax.fori_loop(0, NB // 2, pack_q, 0)

    @pl.when(ctx < 15)
    def _():
        remote(seg_ref.at[0], seg_next, seg_ss, seg_rs, {"ctx": ctx}).wait_recv()

    def column(row):
        return jnp.transpose(jnp.broadcast_to(row.astype(jnp.float32), (TQ, TQ)))

    lane = lax.broadcasted_iota(jnp.int32, (TQ, TQ), 1)
    sub = lax.broadcasted_iota(jnp.int32, (TQ, TQ), 0)
    seg_col = column(seg_row)
    base = jnp.maximum(ctx - (WIN - 1), 0)
    wide = (SEGS, TQ)
    lane_row = lane[:1]
    end_lane = lax.broadcasted_iota(jnp.int32, wide, 1).astype(jnp.float32)
    end_seg = lax.broadcasted_iota(jnp.int32, wide, 0)
    following = jnp.where(
        lane_row == TQ - 1, pltpu.roll(seg_next[...], TQ - 1, 1), pltpu.roll(seg_row, TQ - 1, 1)
    )
    is_end = (following != seg_row) | ((lane_row == TQ - 1) & (ctx == 15))
    pick = jnp.where((seg_row == end_seg) & is_end, 1.0, 0.0)
    end_pos = jnp.sum(pick * end_lane, axis=1, keepdims=True)
    has_end = jnp.sum(pick, axis=1, keepdims=True)
    pick = pick.astype(jnp.bfloat16)
    for h in range(HQ):
        rows = jnp.dot(pick, qs[h], preferred_element_type=jnp.float32).astype(jnp.bfloat16)
        qe[h // GROUP, (h % GROUP) * SEGS : (h % GROUP + 1) * SEGS] = rows

    for c, steps in enumerate(ROUTES):
        @pl.when(ctx == c)
        def _():
            run_steps(c, steps[CUTS[c] :])

    heard(3)
    end_seg_f = end_seg.astype(jnp.float32)
    for w in range(WIN):
        keys = kbuf[base + w, HK * TQ :, :].astype(jnp.float32)
        offset = (base + w - ctx) * TQ
        at = slice(w * TQ, (w + 1) * TQ)
        ends = (keys == end_seg_f) & (end_lane + offset.astype(jnp.float32) <= end_pos)
        bias_end[:, at] = jnp.where(ends, 0.0, NEG)
        allowed = (seg_col == keys[:1]) & (offset + lane <= sub)
        bias[:, at] = jnp.where(allowed, 0.0, NEG)

    def attend(q, g, mask, per, rows):
        part = pl.ds(pl.multiple_of(g * TQ, TQ), TQ)
        k = kbuf[pl.ds(base, WIN), part, :].reshape(WIN * TQ, HD)
        v = vbuf[pl.ds(base, WIN), part, :].reshape(WIN * TQ, HD)
        s = lax.dot_general(q, k, (((1,), (1,)), ((), ())), preferred_element_type=jnp.float32)
        s = (s * SCALE).reshape(per, rows, WIN * TQ) + mask[None]
        top = jnp.max(s, axis=-1, keepdims=True)
        p = jnp.exp2(s - top)
        total = jnp.sum(p, axis=-1, keepdims=True)
        pb = p.astype(jnp.bfloat16).reshape(per * rows, WIN * TQ)
        o = jnp.dot(pb, v, preferred_element_type=jnp.float32).reshape(per, rows, HD)
        return (o / total).astype(jnp.bfloat16)

    terms = jnp.zeros((SEGS, HD), jnp.float32)
    for g in range(HK):
        o = attend(qe[g], g, bias_end[...], GROUP, SEGS)
        for j in range(GROUP):
            h = g * GROUP + j
            terms += o[j].astype(jnp.float32) * rw_ref[h : h + 1, :]
    reward = jnp.where(has_end > 0.5, jnp.sum(terms, axis=1, keepdims=True), 0.0)
    bin_seg = lax.broadcasted_iota(jnp.int32, (SEGS, BINS), 0)
    bin_lane = lax.broadcasted_iota(jnp.int32, (SEGS, BINS), 1)
    bin_of = jnp.zeros((SEGS, BINS), jnp.int32)
    for s in range(SEGS):
        bin_of = jnp.where(bin_seg == s, bins_ref[0, s], bin_of)
    hist_a[dp] = jnp.sum(jnp.where(bin_of == bin_lane, reward, 0.0), axis=0, keepdims=True)

    def out_copy(i):
        at = pl.ds(pl.multiple_of(i * PER * HD, PER * HD), PER * HD)
        return pltpu.make_async_copy(out_ref.at[:, at], out_hbm.at[:, at], out_sem.at[i])

    def heads(i, carry):
        per = PER
        o = attend(qs[pl.ds(i * per, per)].reshape(per * TQ, HD), i // (GROUP // per), bias[...], per, TQ)
        for e in range(per):
            at = pl.ds(pl.multiple_of((i * per + e) * HD, HD), HD)
            out_ref[:, at] = o[e]
        out_copy(i).start()
        return carry

    def hist_copy(buf, ss, rs, axis, me, k):
        return remote(buf.at[me], buf.at[me], ss.at[k], rs.at[me], {axis: (me + k) % 16})

    def hist_start(buf, ss, rs, axis, me):
        def start(k, carry):
            hist_copy(buf, ss, rs, axis, me, k).start()
            return carry

        lax.fori_loop(1, 16, start, 0)

    def hist_total(buf, ss, rs, axis, me):
        def wait(k, carry):
            s = (me + k) % 16
            remote(buf.at[s], buf.at[s], ss.at[k], rs.at[s], {axis: s}).wait_recv()
            return carry

        lax.fori_loop(1, 16, wait, 0)
        return jnp.sum(buf[...], axis=0)

    hist_start(hist_a, ha_ss, ha_rs, "dp", dp)
    lax.fori_loop(0, HALF, heads, 0)
    hist_b[ctx] = hist_total(hist_a, ha_ss, ha_rs, "dp", dp)
    hist_start(hist_b, hb_ss, hb_rs, "ctx", ctx)
    lax.fori_loop(HALF, HQ // PER, heads, 0)
    hist_ref[...] = hist_total(hist_b, hb_ss, hb_rs, "ctx", ctx)

    def drain(k, carry):
        k_copy(k).wait_send()
        v_copy(k).wait_send()
        q_copy(k).wait_send()
        hist_copy(hist_a, ha_ss, ha_rs, "dp", dp, k).wait_send()
        hist_copy(hist_b, hb_ss, hb_rs, "ctx", ctx, k).wait_send()
        return carry

    lax.fori_loop(1, 16, drain, 0)

    @pl.when(ctx > 0)
    def _():
        seg_copy.wait_send()

    def counted(low, high):
        total = jnp.int32(0)
        for c, steps in enumerate(ROUTES):
            total += jnp.where(ctx == c, sum(low <= n < high for n in steps), 0)
        return total

    k_sends = counted(0, 256)

    def drain_items(item):
        def body(slot, carry):
            item_copy(item, ctx, slot).wait_send()
            return carry

        return body

    lax.fori_loop(0, k_sends, drain_items(0), 0)
    lax.fori_loop(k_sends, k_sends + counted(256, 512), drain_items(16), 0)

    def drain_out(i, carry):
        out_copy(i).wait()
        return carry

    lax.fori_loop(0, HQ // PER, drain_out, 0)


def local(roll_query, roll_keys, roll_values, pack_dest, segment_ids, reward_bins, reward_weight):
    vmem = pl.BlockSpec(memory_space=pltpu.VMEM)
    smem = pl.BlockSpec(memory_space=pltpu.SMEM)
    hbm = pl.BlockSpec(memory_space=pltpu.HBM)
    bf16, f32, i32 = jnp.bfloat16, jnp.float32, jnp.int32
    dma = pltpu.SemaphoreType.DMA
    most = max(sum(n >= 0 for n in steps) for steps in ROUTES)
    out, hist = pl.pallas_call(
        kernel,
        out_shape=(jax.ShapeDtypeStruct((TQ, HQ * HD), bf16), jax.ShapeDtypeStruct((1, BINS), f32)),
        in_specs=[smem, smem, hbm, hbm, hbm, vmem, hbm],
        out_specs=(hbm, vmem),
        scratch_shapes=[
            pltpu.VMEM((NB, BLK, HQ * HD), bf16),
            pltpu.VMEM((NB, BLK, HK * HD), bf16),
            pltpu.VMEM((NB, BLK, HK * HD), bf16),
            pltpu.VMEM((HQ, HD), f32),
            pltpu.VMEM((16, BLK, HQ * HD), bf16),
            pltpu.VMEM((16, BLK, HQ * HD), bf16),
            pltpu.VMEM((16, BLK, HK * HD), bf16),
            pltpu.VMEM((16, BLK, HK * HD), bf16),
            pltpu.VMEM((16, BLK, HK * HD), bf16),
            pltpu.VMEM((16, BLK, HK * HD), bf16),
            pltpu.VMEM((HQ, TQ, HD), bf16),
            pltpu.VMEM((HK, GROUP * SEGS, HD), bf16),
            pltpu.VMEM((16, HK * TQ + 16, HD), bf16),
            pltpu.VMEM((16, HK * TQ, HD), bf16),
            pltpu.VMEM((TQ, HQ * HD), bf16),
            pltpu.VMEM((1, TQ), i32),
            pltpu.VMEM((TQ, WIN * TQ), f32),
            pltpu.VMEM((SEGS, WIN * TQ), f32),
            pltpu.VMEM((16, 1, BINS), f32),
            pltpu.VMEM((16, 1, BINS), f32),
            dma((4,)), dma((HQ // PER,)), dma((16,)), dma((16,)), dma((16,)), dma((16,)), dma((16,)), dma((16,)),
            dma, dma, dma((most,)), dma((32,)), dma((16,)), dma((16,)), dma((16,)), dma((16,)),
            pltpu.SemaphoreType.REGULAR((4,)),
        ],
        compiler_params=pltpu.CompilerParams(
            collective_id=0, has_side_effects=True, vmem_limit_bytes=60 * 1024 * 1024
        ),
    )(
        pack_dest,
        reward_bins,
        roll_query.reshape(NB, BLK, HQ * HD),
        roll_keys.reshape(NB, BLK, HK * HD),
        roll_values.reshape(NB, BLK, HK * HD),
        segment_ids.reshape(1, 1, TQ),
        reward_weight.reshape(HQ, HD),
    )
    return out.reshape(1, TQ, HQ * HD), hist.reshape(BINS)


def solution(mesh):
    in_specs = (
        P("dp", "ctx", None),
        P("dp", "ctx", None),
        P("dp", "ctx", None),
        P(None, "ctx"),
        P("dp", "ctx"),
        P("dp", None),
        P(),
    )
    out_specs = (P("dp", "ctx", None), P())
    return jax.shard_map(local, mesh=mesh, in_specs=in_specs, out_specs=out_specs, check_vma=False)
```

```python
import functools
import math

import jax
import jax.numpy as jnp
from jax import lax
from jax.experimental import pallas as pl
from jax.experimental.pallas import tpu as pltpu
from jax.sharding import PartitionSpec as P

HQ = 32
HK = 4
HD = 128
TQ = 128
BLK = 8
NB = 16
SEGS = 16
BINS = 512
GROUP = HQ // HK
WIN = 9
PER = 2
HALF = 8
NEG = -1e30
SCALE = math.log2(math.e) / math.sqrt(HD)
MESH = pl.DeviceIdType.MESH

ROUTES = (
    (264, 7, 1, 263, 257, -18, 8, 279, -2, -7, 104, 23, -19, 295, -3, 24, -22, 39, 337, -20, 344, 311, 312),
    (272, 281, 18, 16, 274, -1, -19, 297, 288, 2, -17, -3, 32, 25, 258, -20, 304, 313, -22, 345),
    (35, 42, 289, 291, 33, -20, -2, 314, 19, 305, -18, -21, 275, 330, -1, 3, -6, -17, 90, 259, -7, 106),
    (306, 52, 59, 308, -21, -3, 322, 331, 36, -19, -6, 82, 292, 91, -2, 20, -7, -18, 98, 107, 276, -1, 315, -17),
    (323, 76, 325, 69, -4, -6, 83, 92, 53, -20, -7, 99, 108, 309, -3, 37, -19, -24, 380, 293, -2, -1, 332, -18, -17),
    (84, 349, 342, 86, -7, -21, 100, 109, 326, -5, -24, 372, 381, 70, -4, 54, -1, -20, 4, 93, 310, -17, -3, 260, 38, -18, -19, -2),
    (101, 366, 103, 359, -24, -22, 373, 382, 343, -6, -1, 5, 110, 87, -21, -17, 261, 327, -5, -18, 277, 71, -4, -2, 21, 55, -20, -19, -3),
    (374, 127, -1, -7, 6, 96, 383, -17, -23, 262, 367, -18, -22, 278, 336, -2, -6, 22, 95, -19, -21, 294, -3, -5, -20, -4),
    (393, 143, 137, 399, -10, 159, -17, -26, 415, -11, -1, -8, 121, 175, -18, -7, -24, -19, 377, -3, 105, -2, -23, -4, 361, -22, -6, -21, -5, -20),
    (410, 152, 154, 408, -25, -11, 394, 168, -18, -9, 138, 280, -19, -3, 298, 296, 40, -2, -8, -4, 122, 56, -20, -24, -21, 378, 328, -7, -5, 72, -22, -23, -6),
    (169, 427, 171, -26, 411, -3, -10, 41, 155, -25, -20, -4, 57, 395, -9, 139, -21, -19, -5, 329, 73, -6, -8, -22, 123, 89, -7, -24, -23),
    (444, 188, -27, 428, -4, -11, 58, 172, -26, -21, -5, 412, 74, -10, 156, -6, -22, -25, 346, 396, -9, -7, -23, 362, -20, -24, -8),
    (205, 461, -28, 445, -5, -12, 75, 189, -27, -6, -22, 347, 429, -11, 173, -7, -23, -26, 363, 413, -9, -10, -24, 379, -8, -25, -21),
    (222, 478, -13, 206, -22, -29, 348, 462, -28, -7, -23, 446, 364, -12, -9, 190, 140, -24, -27, -8, 430, 124, -11, -6, -10, -26, -25),
    (239, 495, -14, 223, -23, -30, 365, -9, 479, -13, 141, -24, -8, 207, -29, 125, -10, 463, -7, -28, 157, -25, 447, -12, 397, -11, 191, -27, -26, 431),
    (-9, -15, 142, -8, -25, -31, 120, 126, -10, -14, 158, -24, 376, -26, -30, 398, -23, -11, -13, 360, 174, -29, 414, -6, 88, -28, -12, -27),
)
CUTS = (22, 20, 22, 24, 25, 28, 29, 26, 24, 27, 25, 24, 26, 26, 28, 26)


def remote(src, dst, send_sem, recv_sem, device_id):
    return pltpu.make_async_remote_copy(
        src_ref=src, dst_ref=dst, send_sem=send_sem, recv_sem=recv_sem, device_id=device_id, device_id_type=MESH
    )


def kernel(
    dest_ref, bins_ref, rq_hbm, rk_hbm, rv_hbm, seg_ref, rw_hbm,
    out_ref, hist_ref,
    rq_ref, rk_ref, rv_ref, rw_ref, qsend, qrecv, ksend, krecv, vsend, vrecv, qs, qe, kbuf, vbuf, seg_next,
    bias, bias_end, hist_a, hist_b,
    in_sem, q_ss, q_rs, k_ss, k_rs, v_ss, v_rs, seg_ss, seg_rs, item_ss, item_rs,
    ha_ss, ha_rs, hb_ss, hb_rs, known,
):
    dp = lax.axis_index("dp")
    ctx = lax.axis_index("ctx")
    line = ctx // 8 * 8
    near = (line + (ctx + 1) % 8, line + (ctx + 7) % 8, (ctx + 8) % 16)
    loads = [
        pltpu.make_async_copy(src, dst, in_sem.at[i])
        for i, (src, dst) in enumerate(
            ((rk_hbm, rk_ref), (rv_hbm, rv_ref), (rq_hbm, rq_ref), (rw_hbm, rw_ref))
        )
    ]
    barrier = pltpu.get_barrier_semaphore()

    def greet(k, carry):
        pl.semaphore_signal(barrier, inc=1, device_id={"dp": (dp + k) % 16}, device_id_type=MESH)
        return carry

    lax.fori_loop(1, 16, greet, 0)
    for to in near:
        pl.semaphore_signal(barrier, inc=1, device_id={"ctx": to}, device_id_type=MESH)

    @pl.when(ctx == 7)
    def _():
        pl.semaphore_signal(barrier, inc=1, device_id={"ctx": 8}, device_id_type=MESH)

    for load in loads:
        load.start()

    def fill(src, dst):
        def body(d, carry):
            inv = jnp.int32(0)
            for j in range(NB):
                inv = jnp.where(dest_ref[dp, j] == d, j, inv)
            dst[d] = src[inv]
            return carry

        lax.fori_loop(0, NB, body, 0)

    def exchange(send, recv, ss, rs):
        def copy(k):
            d = (dp + k) % 16
            return remote(send.at[d], recv.at[dp], ss.at[k], rs.at[dp], {"dp": d})

        def start(k, carry):
            copy(k).start()
            return carry

        def wait(k, carry):
            s = (dp + k) % 16
            remote(send.at[s], recv.at[s], ss.at[k], rs.at[s], {"dp": s}).wait_recv()
            return carry

        return copy, start, wait

    k_copy, k_start, k_wait = exchange(ksend, krecv, k_ss, k_rs)
    v_copy, v_start, v_wait = exchange(vsend, vrecv, v_ss, v_rs)
    q_copy, q_start, q_wait = exchange(qsend, qrecv, q_ss, q_rs)
    loads[0].wait()
    fill(rk_ref, ksend)
    loads[1].wait()
    fill(rv_ref, vsend)
    pl.semaphore_wait(barrier, 18 + jnp.where(ctx == 8, 1, 0))
    lax.fori_loop(1, 16, k_start, 0)
    lax.fori_loop(1, 16, v_start, 0)
    krecv[dp] = ksend[dp]
    vrecv[dp] = vsend[dp]

    def spread(r):
        for to in near:
            pl.semaphore_signal(known.at[r], inc=1, device_id={"ctx": to}, device_id_type=MESH)

    def heard(r):
        pl.semaphore_wait(known.at[r], 3)

    seg_copy = remote(seg_ref.at[0], seg_next, seg_ss, seg_rs, {"ctx": (ctx + 15) % 16})
    spread(0)

    @pl.when(ctx > 0)
    def _():
        seg_copy.start()

    loads[2].wait()
    fill(rq_ref, qsend)
    loads[3].wait()
    heard(0)
    spread(1)

    def source_of(j):
        src = jnp.int32(0)
        for s in range(16):
            src = jnp.where(dest_ref[s, j] == dp, s, src)
        return src

    def rows_of(recv, jj):
        top = recv[source_of(2 * jj)].astype(jnp.float32)
        low = recv[source_of(2 * jj + 1)].astype(jnp.float32)
        return jnp.concatenate([top, low], axis=0).astype(jnp.bfloat16)

    def pack(recv, buf):
        def body(jj, carry):
            rows = rows_of(recv, jj)
            for g in range(HK):
                at = pl.ds(pl.multiple_of(g * TQ + jj * 16, 16), 16)
                buf[ctx, at, :] = rows[:, g * HD : (g + 1) * HD]
            return carry

        lax.fori_loop(0, NB // 2, body, 0)

    def item_copy(item, to, slot):
        buf = (kbuf, vbuf)[item // 16].at[item % 16]
        return remote(buf, buf, item_ss.at[slot], item_rs.at[item], {"ctx": to})

    slots = []
    for steps in ROUTES:
        k_sends = [n for n in steps if 0 <= n < 256]
        v_sends = [n for n in steps if n >= 256]
        slots.append({n: i for i, n in enumerate(k_sends + v_sends)})

    def run_steps(c, steps):
        for n in steps:
            if n < 0:
                item_copy(-1 - n, ctx, 0).wait_recv()
            else:
                item_copy(n // 16, n % 16, slots[c][n]).start()

    first = [next((i for i, n in enumerate(steps) if n < 0), len(steps)) for steps in ROUTES]
    seg_row = seg_ref[0]
    kbuf[ctx, HK * TQ :, :] = jnp.broadcast_to(seg_row.astype(jnp.float32), (16, TQ)).astype(jnp.bfloat16)
    lax.fori_loop(1, 16, k_wait, 0)
    pack(krecv, kbuf)
    for c, steps in enumerate(ROUTES):
        @pl.when(ctx == c)
        def _():
            run_steps(c, [n for n in steps[: first[c]] if n < 256])

    lax.fori_loop(1, 16, v_wait, 0)
    pack(vrecv, vbuf)
    for c, steps in enumerate(ROUTES):
        @pl.when(ctx == c)
        def _():
            run_steps(c, [n for n in steps[: first[c]] if n >= 256])

    lax.fori_loop(1, 16, q_start, 0)
    qrecv[dp] = qsend[dp]
    heard(1)
    spread(2)
    for c, steps in enumerate(ROUTES):
        @pl.when(ctx == c)
        def _():
            for b in range(c + 1, WIN):
                if -1 - b not in steps:
                    kbuf[b] = jnp.zeros((HK * TQ + 16, HD), jnp.bfloat16)
                if -1 - (16 + b) not in steps:
                    vbuf[b] = jnp.zeros((HK * TQ, HD), jnp.bfloat16)
            run_steps(c, steps[first[c] : CUTS[c]])

    heard(2)
    spread(3)
    lax.fori_loop(1, 16, q_wait, 0)

    def pack_q(jj, carry):
        rows = rows_of(qrecv, jj)
        at = pl.ds(pl.multiple_of(jj * 16, 16), 16)
        for h in range(HQ):
            qs[h, at, :] = rows[:, h * HD : (h + 1) * HD]
        return carry

    lax.fori_loop(0, NB // 2, pack_q, 0)

    @pl.when(ctx < 15)
    def _():
        remote(seg_ref.at[0], seg_next, seg_ss, seg_rs, {"ctx": ctx}).wait_recv()

    def column(row):
        return jnp.transpose(jnp.broadcast_to(row.astype(jnp.float32), (TQ, TQ)))

    lane = lax.broadcasted_iota(jnp.int32, (TQ, TQ), 1)
    sub = lax.broadcasted_iota(jnp.int32, (TQ, TQ), 0)
    seg_col = column(seg_row)
    base = jnp.maximum(ctx - (WIN - 1), 0)
    wide = (SEGS, TQ)
    lane_row = lane[:1]
    end_lane = lax.broadcasted_iota(jnp.int32, wide, 1).astype(jnp.float32)
    end_seg = lax.broadcasted_iota(jnp.int32, wide, 0)
    following = jnp.where(
        lane_row == TQ - 1, pltpu.roll(seg_next[...], TQ - 1, 1), pltpu.roll(seg_row, TQ - 1, 1)
    )
    is_end = (following != seg_row) | ((lane_row == TQ - 1) & (ctx == 15))
    pick = jnp.where((seg_row == end_seg) & is_end, 1.0, 0.0)
    end_pos = jnp.sum(pick * end_lane, axis=1, keepdims=True)
    has_end = jnp.sum(pick, axis=1, keepdims=True)
    pick = pick.astype(jnp.bfloat16)
    for h in range(HQ):
        rows = jnp.dot(pick, qs[h], preferred_element_type=jnp.float32).astype(jnp.bfloat16)
        qe[h // GROUP, (h % GROUP) * SEGS : (h % GROUP + 1) * SEGS] = rows

    for c, steps in enumerate(ROUTES):
        @pl.when(ctx == c)
        def _():
            run_steps(c, steps[CUTS[c] :])

    heard(3)
    end_seg_f = end_seg.astype(jnp.float32)
    for w in range(WIN):
        keys = kbuf[base + w, HK * TQ :, :].astype(jnp.float32)
        offset = (base + w - ctx) * TQ
        at = slice(w * TQ, (w + 1) * TQ)
        ends = (keys == end_seg_f) & (end_lane + offset.astype(jnp.float32) <= end_pos)
        bias_end[:, at] = jnp.where(ends, 0.0, NEG)
        allowed = (seg_col == keys[:1]) & (offset + lane <= sub)
        bias[:, at] = jnp.where(allowed, 0.0, NEG)

    def attend(q, g, mask, per, rows):
        part = pl.ds(pl.multiple_of(g * TQ, TQ), TQ)
        k = kbuf[pl.ds(base, WIN), part, :].reshape(WIN * TQ, HD)
        v = vbuf[pl.ds(base, WIN), part, :].reshape(WIN * TQ, HD)
        s = lax.dot_general(q, k, (((1,), (1,)), ((), ())), preferred_element_type=jnp.float32)
        s = (s * SCALE).reshape(per, rows, WIN * TQ) + mask[None]
        top = jnp.max(s, axis=-1, keepdims=True)
        p = jnp.exp2(s - top)
        total = jnp.sum(p, axis=-1, keepdims=True)
        pb = p.astype(jnp.bfloat16).reshape(per * rows, WIN * TQ)
        o = jnp.dot(pb, v, preferred_element_type=jnp.float32).reshape(per, rows, HD)
        return (o / total).astype(jnp.bfloat16)

    terms = jnp.zeros((SEGS, HD), jnp.float32)
    for g in range(HK):
        o = attend(qe[g], g, bias_end[...], GROUP, SEGS)
        for j in range(GROUP):
            h = g * GROUP + j
            terms += o[j].astype(jnp.float32) * rw_ref[h : h + 1, :]
    reward = jnp.where(has_end > 0.5, jnp.sum(terms, axis=1, keepdims=True), 0.0)
    bin_seg = lax.broadcasted_iota(jnp.int32, (SEGS, BINS), 0)
    bin_lane = lax.broadcasted_iota(jnp.int32, (SEGS, BINS), 1)
    bin_of = jnp.zeros((SEGS, BINS), jnp.int32)
    for s in range(SEGS):
        bin_of = jnp.where(bin_seg == s, bins_ref[0, s], bin_of)
    hist_a[dp] = jnp.sum(jnp.where(bin_of == bin_lane, reward, 0.0), axis=0, keepdims=True)

    def heads(i, carry):
        per = PER
        o = attend(qs[pl.ds(i * per, per)].reshape(per * TQ, HD), i // (GROUP // per), bias[...], per, TQ)
        for e in range(per):
            at = pl.ds(pl.multiple_of((i * per + e) * HD, HD), HD)
            out_ref[:, at] = o[e]
        return carry

    def hist_copy(buf, ss, rs, axis, me, k):
        return remote(buf.at[me], buf.at[me], ss.at[k], rs.at[me], {axis: (me + k) % 16})

    def hist_start(buf, ss, rs, axis, me):
        def start(k, carry):
            hist_copy(buf, ss, rs, axis, me, k).start()
            return carry

        lax.fori_loop(1, 16, start, 0)

    def hist_total(buf, ss, rs, axis, me):
        def wait(k, carry):
            s = (me + k) % 16
            remote(buf.at[s], buf.at[s], ss.at[k], rs.at[s], {axis: s}).wait_recv()
            return carry

        lax.fori_loop(1, 16, wait, 0)
        return jnp.sum(buf[...], axis=0)

    hist_start(hist_a, ha_ss, ha_rs, "dp", dp)
    lax.fori_loop(0, HALF, heads, 0)
    hist_b[ctx] = hist_total(hist_a, ha_ss, ha_rs, "dp", dp)
    hist_start(hist_b, hb_ss, hb_rs, "ctx", ctx)
    lax.fori_loop(HALF, HQ // PER, heads, 0)
    hist_ref[...] = hist_total(hist_b, hb_ss, hb_rs, "ctx", ctx)

    def drain(k, carry):
        k_copy(k).wait_send()
        v_copy(k).wait_send()
        q_copy(k).wait_send()
        hist_copy(hist_a, ha_ss, ha_rs, "dp", dp, k).wait_send()
        hist_copy(hist_b, hb_ss, hb_rs, "ctx", ctx, k).wait_send()
        return carry

    lax.fori_loop(1, 16, drain, 0)

    @pl.when(ctx > 0)
    def _():
        seg_copy.wait_send()

    def counted(low, high):
        total = jnp.int32(0)
        for c, steps in enumerate(ROUTES):
            total += jnp.where(ctx == c, sum(low <= n < high for n in steps), 0)
        return total

    k_sends = counted(0, 256)

    def drain_items(item):
        def body(slot, carry):
            item_copy(item, ctx, slot).wait_send()
            return carry

        return body

    lax.fori_loop(0, k_sends, drain_items(0), 0)
    lax.fori_loop(k_sends, k_sends + counted(256, 512), drain_items(16), 0)


def local(roll_query, roll_keys, roll_values, pack_dest, segment_ids, reward_bins, reward_weight):
    vmem = pl.BlockSpec(memory_space=pltpu.VMEM)
    smem = pl.BlockSpec(memory_space=pltpu.SMEM)
    hbm = pl.BlockSpec(memory_space=pltpu.HBM)
    bf16, f32, i32 = jnp.bfloat16, jnp.float32, jnp.int32
    dma = pltpu.SemaphoreType.DMA
    most = max(sum(n >= 0 for n in steps) for steps in ROUTES)
    out, hist = pl.pallas_call(
        kernel,
        out_shape=(pltpu.VMEM((TQ, HQ * HD), bf16), pltpu.VMEM((1, BINS), f32)),
        in_specs=[smem, smem, hbm, hbm, hbm, vmem, hbm],
        out_specs=(vmem, vmem),
        scratch_shapes=[
            pltpu.VMEM((NB, BLK, HQ * HD), bf16),
            pltpu.VMEM((NB, BLK, HK * HD), bf16),
            pltpu.VMEM((NB, BLK, HK * HD), bf16),
            pltpu.VMEM((HQ, HD), f32),
            pltpu.VMEM((16, BLK, HQ * HD), bf16),
            pltpu.VMEM((16, BLK, HQ * HD), bf16),
            pltpu.VMEM((16, BLK, HK * HD), bf16),
            pltpu.VMEM((16, BLK, HK * HD), bf16),
            pltpu.VMEM((16, BLK, HK * HD), bf16),
            pltpu.VMEM((16, BLK, HK * HD), bf16),
            pltpu.VMEM((HQ, TQ, HD), bf16),
            pltpu.VMEM((HK, GROUP * SEGS, HD), bf16),
            pltpu.VMEM((16, HK * TQ + 16, HD), bf16),
            pltpu.VMEM((16, HK * TQ, HD), bf16),
            pltpu.VMEM((1, TQ), i32),
            pltpu.VMEM((TQ, WIN * TQ), f32),
            pltpu.VMEM((SEGS, WIN * TQ), f32),
            pltpu.VMEM((16, 1, BINS), f32),
            pltpu.VMEM((16, 1, BINS), f32),
            dma((4,)), dma((16,)), dma((16,)), dma((16,)), dma((16,)), dma((16,)), dma((16,)),
            dma, dma, dma((most,)), dma((32,)), dma((16,)), dma((16,)), dma((16,)), dma((16,)),
            pltpu.SemaphoreType.REGULAR((4,)),
        ],
        compiler_params=pltpu.CompilerParams(
            collective_id=0, has_side_effects=True, vmem_limit_bytes=56 * 1024 * 1024
        ),
    )(
        pack_dest,
        reward_bins,
        roll_query.reshape(NB, BLK, HQ * HD),
        roll_keys.reshape(NB, BLK, HK * HD),
        roll_values.reshape(NB, BLK, HK * HD),
        segment_ids.reshape(1, 1, TQ),
        reward_weight.reshape(HQ, HD),
    )
    return out.reshape(1, TQ, HQ * HD), hist.reshape(BINS)


def solution(mesh):
    in_specs = (
        P("dp", "ctx", None),
        P("dp", "ctx", None),
        P("dp", "ctx", None),
        P(None, "ctx"),
        P("dp", "ctx"),
        P("dp", None),
        P(),
    )
    out_specs = (P("dp", "ctx", None), P())
    return jax.shard_map(local, mesh=mesh, in_specs=in_specs, out_specs=out_specs, check_vma=False)
```

```python
import functools
import math

import jax
import jax.numpy as jnp
from jax import lax
from jax.experimental import pallas as pl
from jax.experimental.pallas import tpu as pltpu
from jax.sharding import PartitionSpec as P

HQ = 32
HK = 4
HD = 128
TQ = 128
BLK = 8
NB = 16
SEGS = 16
BINS = 512
GROUP = HQ // HK
WIN = 9
PER = 2
HALF = 8
NEG = -1e30
SCALE = math.log2(math.e) / math.sqrt(HD)
MESH = pl.DeviceIdType.MESH

ROUTES = (
    (264, 7, 1, 263, 257, -18, 8, 279, -2, -7, 104, 23, -19, 295, -3, 24, -22, 39, 337, -20, 344, 311, 312),
    (272, 281, 18, 16, 274, -1, -19, 297, 288, 2, -17, -3, 32, 25, 258, -20, 304, 313, -22, 345),
    (35, 42, 289, 291, 33, -20, -2, 314, 19, 305, -18, -21, 275, 330, -1, 3, -6, -17, 90, 259, -7, 106),
    (306, 52, 59, 308, -21, -3, 322, 331, 36, -19, -6, 82, 292, 91, -2, 20, -7, -18, 98, 107, 276, -1, 315, -17),
    (323, 76, 325, 69, -4, -6, 83, 92, 53, -20, -7, 99, 108, 309, -3, 37, -19, -24, 380, 293, -2, -1, 332, -18, -17),
    (84, 349, 342, 86, -7, -21, 100, 109, 326, -5, -24, 372, 381, 70, -4, 54, -1, -20, 4, 93, 310, -17, -3, 260, 38, -18, -19, -2),
    (101, 366, 103, 359, -24, -22, 373, 382, 343, -6, -1, 5, 110, 87, -21, -17, 261, 327, -5, -18, 277, 71, -4, -2, 21, 55, -20, -19, -3),
    (374, 127, -1, -7, 6, 96, 383, -17, -23, 262, 367, -18, -22, 278, 336, -2, -6, 22, 95, -19, -21, 294, -3, -5, -20, -4),
    (393, 143, 137, 399, -10, 159, -17, -26, 415, -11, -1, -8, 121, 175, -18, -7, -24, -19, 377, -3, 105, -2, -23, -4, 361, -22, -6, -21, -5, -20),
    (410, 152, 154, 408, -25, -11, 394, 168, -18, -9, 138, 280, -19, -3, 298, 296, 40, -2, -8, -4, 122, 56, -20, -24, -21, 378, 328, -7, -5, 72, -22, -23, -6),
    (169, 427, 171, -26, 411, -3, -10, 41, 155, -25, -20, -4, 57, 395, -9, 139, -21, -19, -5, 329, 73, -6, -8, -22, 123, 89, -7, -24, -23),
    (444, 188, -27, 428, -4, -11, 58, 172, -26, -21, -5, 412, 74, -10, 156, -6, -22, -25, 346, 396, -9, -7, -23, 362, -20, -24, -8),
    (205, 461, -28, 445, -5, -12, 75, 189, -27, -6, -22, 347, 429, -11, 173, -7, -23, -26, 363, 413, -9, -10, -24, 379, -8, -25, -21),
    (222, 478, -13, 206, -22, -29, 348, 462, -28, -7, -23, 446, 364, -12, -9, 190, 140, -24, -27, -8, 430, 124, -11, -6, -10, -26, -25),
    (239, 495, -14, 223, -23, -30, 365, -9, 479, -13, 141, -24, -8, 207, -29, 125, -10, 463, -7, -28, 157, -25, 447, -12, 397, -11, 191, -27, -26, 431),
    (-9, -15, 142, -8, -25, -31, 120, 126, -10, -14, 158, -24, 376, -26, -30, 398, -23, -11, -13, 360, 174, -29, 414, -6, 88, -28, -12, -27),
)
CUTS = (22, 20, 22, 24, 25, 28, 29, 26, 24, 27, 25, 24, 26, 26, 28, 26)


def remote(src, dst, send_sem, recv_sem, device_id):
    return pltpu.make_async_remote_copy(
        src_ref=src, dst_ref=dst, send_sem=send_sem, recv_sem=recv_sem, device_id=device_id, device_id_type=MESH
    )


def kernel(
    dest_hbm, bins_hbm, rq_hbm, rk_hbm, rv_hbm, seg_hbm, rw_hbm,
    out_ref, hist_ref,
    dest_ref, bins_ref, seg_ref, rq_ref, rk_ref, rv_ref, rw_ref, qsend, qrecv, ksend, krecv, vsend, vrecv, qs, qe, kbuf, vbuf, seg_next,
    bias, bias_end, hist_a, hist_b,
    in_sem, q_ss, q_rs, k_ss, k_rs, v_ss, v_rs, seg_ss, seg_rs, item_ss, item_rs,
    ha_ss, ha_rs, hb_ss, hb_rs, known,
):
    dp = lax.axis_index("dp")
    ctx = lax.axis_index("ctx")
    line = ctx // 8 * 8
    near = (line + (ctx + 1) % 8, line + (ctx + 7) % 8, (ctx + 8) % 16)
    loads = [
        pltpu.make_async_copy(src, dst, in_sem.at[i])
        for i, (src, dst) in enumerate(
            (
                (dest_hbm, dest_ref), (rk_hbm, rk_ref), (rv_hbm, rv_ref), (seg_hbm, seg_ref),
                (bins_hbm, bins_ref), (rq_hbm, rq_ref), (rw_hbm, rw_ref),
            )
        )
    ]
    barrier = pltpu.get_barrier_semaphore()

    def greet(k, carry):
        pl.semaphore_signal(barrier, inc=1, device_id={"dp": (dp + k) % 16}, device_id_type=MESH)
        return carry

    lax.fori_loop(1, 16, greet, 0)
    for to in near:
        pl.semaphore_signal(barrier, inc=1, device_id={"ctx": to}, device_id_type=MESH)

    @pl.when(ctx == 7)
    def _():
        pl.semaphore_signal(barrier, inc=1, device_id={"ctx": 8}, device_id_type=MESH)

    for load in loads:
        load.start()

    def fill(src, dst):
        def body(d, carry):
            inv = jnp.int32(0)
            for j in range(NB):
                inv = jnp.where(dest_ref[dp, j] == d, j, inv)
            dst[d] = src[inv]
            return carry

        lax.fori_loop(0, NB, body, 0)

    def exchange(send, recv, ss, rs):
        def copy(k):
            d = (dp + k) % 16
            return remote(send.at[d], recv.at[dp], ss.at[k], rs.at[dp], {"dp": d})

        def start(k, carry):
            copy(k).start()
            return carry

        def wait(k, carry):
            s = (dp + k) % 16
            remote(send.at[s], recv.at[s], ss.at[k], rs.at[s], {"dp": s}).wait_recv()
            return carry

        return copy, start, wait

    k_copy, k_start, k_wait = exchange(ksend, krecv, k_ss, k_rs)
    v_copy, v_start, v_wait = exchange(vsend, vrecv, v_ss, v_rs)
    q_copy, q_start, q_wait = exchange(qsend, qrecv, q_ss, q_rs)
    loads[0].wait()
    loads[1].wait()
    fill(rk_ref, ksend)
    loads[2].wait()
    fill(rv_ref, vsend)
    pl.semaphore_wait(barrier, 18 + jnp.where(ctx == 8, 1, 0))
    lax.fori_loop(1, 16, k_start, 0)
    lax.fori_loop(1, 16, v_start, 0)
    krecv[dp] = ksend[dp]
    vrecv[dp] = vsend[dp]

    def spread(r):
        for to in near:
            pl.semaphore_signal(known.at[r], inc=1, device_id={"ctx": to}, device_id_type=MESH)

    def heard(r):
        pl.semaphore_wait(known.at[r], 3)

    loads[3].wait()
    loads[4].wait()
    seg_copy = remote(seg_ref.at[0], seg_next, seg_ss, seg_rs, {"ctx": (ctx + 15) % 16})
    spread(0)

    @pl.when(ctx > 0)
    def _():
        seg_copy.start()

    loads[5].wait()
    fill(rq_ref, qsend)
    loads[6].wait()
    heard(0)
    spread(1)

    def source_of(j):
        src = jnp.int32(0)
        for s in range(16):
            src = jnp.where(dest_ref[s, j] == dp, s, src)
        return src

    def rows_of(recv, jj):
        top = recv[source_of(2 * jj)].astype(jnp.float32)
        low = recv[source_of(2 * jj + 1)].astype(jnp.float32)
        return jnp.concatenate([top, low], axis=0).astype(jnp.bfloat16)

    def pack(recv, buf):
        def body(jj, carry):
            rows = rows_of(recv, jj)
            for g in range(HK):
                at = pl.ds(pl.multiple_of(g * TQ + jj * 16, 16), 16)
                buf[ctx, at, :] = rows[:, g * HD : (g + 1) * HD]
            return carry

        lax.fori_loop(0, NB // 2, body, 0)

    def item_copy(item, to, slot):
        buf = (kbuf, vbuf)[item // 16].at[item % 16]
        return remote(buf, buf, item_ss.at[slot], item_rs.at[item], {"ctx": to})

    slots = []
    for steps in ROUTES:
        k_sends = [n for n in steps if 0 <= n < 256]
        v_sends = [n for n in steps if n >= 256]
        slots.append({n: i for i, n in enumerate(k_sends + v_sends)})

    def run_steps(c, steps):
        for n in steps:
            if n < 0:
                item_copy(-1 - n, ctx, 0).wait_recv()
            else:
                item_copy(n // 16, n % 16, slots[c][n]).start()

    first = [next((i for i, n in enumerate(steps) if n < 0), len(steps)) for steps in ROUTES]
    seg_row = seg_ref[0]
    kbuf[ctx, HK * TQ :, :] = jnp.broadcast_to(seg_row.astype(jnp.float32), (16, TQ)).astype(jnp.bfloat16)
    lax.fori_loop(1, 16, k_wait, 0)
    pack(krecv, kbuf)
    for c, steps in enumerate(ROUTES):
        @pl.when(ctx == c)
        def _():
            run_steps(c, [n for n in steps[: first[c]] if n < 256])

    lax.fori_loop(1, 16, v_wait, 0)
    pack(vrecv, vbuf)
    for c, steps in enumerate(ROUTES):
        @pl.when(ctx == c)
        def _():
            run_steps(c, [n for n in steps[: first[c]] if n >= 256])

    lax.fori_loop(1, 16, q_start, 0)
    qrecv[dp] = qsend[dp]
    heard(1)
    spread(2)
    for c, steps in enumerate(ROUTES):
        @pl.when(ctx == c)
        def _():
            for b in range(c + 1, WIN):
                if -1 - b not in steps:
                    kbuf[b] = jnp.zeros((HK * TQ + 16, HD), jnp.bfloat16)
                if -1 - (16 + b) not in steps:
                    vbuf[b] = jnp.zeros((HK * TQ, HD), jnp.bfloat16)
            run_steps(c, steps[first[c] : CUTS[c]])

    heard(2)
    spread(3)
    lax.fori_loop(1, 16, q_wait, 0)

    def pack_q(jj, carry):
        rows = rows_of(qrecv, jj)
        at = pl.ds(pl.multiple_of(jj * 16, 16), 16)
        for h in range(HQ):
            qs[h, at, :] = rows[:, h * HD : (h + 1) * HD]
        return carry

    lax.fori_loop(0, NB // 2, pack_q, 0)

    @pl.when(ctx < 15)
    def _():
        remote(seg_ref.at[0], seg_next, seg_ss, seg_rs, {"ctx": ctx}).wait_recv()

    def column(row):
        return jnp.transpose(jnp.broadcast_to(row.astype(jnp.float32), (TQ, TQ)))

    lane = lax.broadcasted_iota(jnp.int32, (TQ, TQ), 1)
    sub = lax.broadcasted_iota(jnp.int32, (TQ, TQ), 0)
    seg_col = column(seg_row)
    base = jnp.maximum(ctx - (WIN - 1), 0)
    wide = (SEGS, TQ)
    lane_row = lane[:1]
    end_lane = lax.broadcasted_iota(jnp.int32, wide, 1).astype(jnp.float32)
    end_seg = lax.broadcasted_iota(jnp.int32, wide, 0)
    following = jnp.where(
        lane_row == TQ - 1, pltpu.roll(seg_next[...], TQ - 1, 1), pltpu.roll(seg_row, TQ - 1, 1)
    )
    is_end = (following != seg_row) | ((lane_row == TQ - 1) & (ctx == 15))
    pick = jnp.where((seg_row == end_seg) & is_end, 1.0, 0.0)
    end_pos = jnp.sum(pick * end_lane, axis=1, keepdims=True)
    has_end = jnp.sum(pick, axis=1, keepdims=True)
    pick = pick.astype(jnp.bfloat16)
    for h in range(HQ):
        rows = jnp.dot(pick, qs[h], preferred_element_type=jnp.float32).astype(jnp.bfloat16)
        qe[h // GROUP, (h % GROUP) * SEGS : (h % GROUP + 1) * SEGS] = rows

    for c, steps in enumerate(ROUTES):
        @pl.when(ctx == c)
        def _():
            run_steps(c, steps[CUTS[c] :])

    heard(3)
    end_seg_f = end_seg.astype(jnp.float32)
    for w in range(WIN):
        keys = kbuf[base + w, HK * TQ :, :].astype(jnp.float32)
        offset = (base + w - ctx) * TQ
        at = slice(w * TQ, (w + 1) * TQ)
        ends = (keys == end_seg_f) & (end_lane + offset.astype(jnp.float32) <= end_pos)
        bias_end[:, at] = jnp.where(ends, 0.0, NEG)
        allowed = (seg_col == keys[:1]) & (offset + lane <= sub)
        bias[:, at] = jnp.where(allowed, 0.0, NEG)

    def attend(q, g, mask, per, rows):
        part = pl.ds(pl.multiple_of(g * TQ, TQ), TQ)
        k = kbuf[pl.ds(base, WIN), part, :].reshape(WIN * TQ, HD)
        v = vbuf[pl.ds(base, WIN), part, :].reshape(WIN * TQ, HD)
        s = lax.dot_general(q, k, (((1,), (1,)), ((), ())), preferred_element_type=jnp.float32)
        s = (s * SCALE).reshape(per, rows, WIN * TQ) + mask[None]
        top = jnp.max(s, axis=-1, keepdims=True)
        p = jnp.exp2(s - top)
        total = jnp.sum(p, axis=-1, keepdims=True)
        pb = p.astype(jnp.bfloat16).reshape(per * rows, WIN * TQ)
        o = jnp.dot(pb, v, preferred_element_type=jnp.float32).reshape(per, rows, HD)
        return (o / total).astype(jnp.bfloat16)

    terms = jnp.zeros((SEGS, HD), jnp.float32)
    for g in range(HK):
        o = attend(qe[g], g, bias_end[...], GROUP, SEGS)
        for j in range(GROUP):
            h = g * GROUP + j
            terms += o[j].astype(jnp.float32) * rw_ref[h : h + 1, :]
    reward = jnp.where(has_end > 0.5, jnp.sum(terms, axis=1, keepdims=True), 0.0)
    bin_seg = lax.broadcasted_iota(jnp.int32, (SEGS, BINS), 0)
    bin_lane = lax.broadcasted_iota(jnp.int32, (SEGS, BINS), 1)
    bin_of = jnp.zeros((SEGS, BINS), jnp.int32)
    for s in range(SEGS):
        bin_of = jnp.where(bin_seg == s, bins_ref[0, s], bin_of)
    hist_a[dp] = jnp.sum(jnp.where(bin_of == bin_lane, reward, 0.0), axis=0, keepdims=True)

    def heads(i, carry):
        per = PER
        o = attend(qs[pl.ds(i * per, per)].reshape(per * TQ, HD), i // (GROUP // per), bias[...], per, TQ)
        for e in range(per):
            at = pl.ds(pl.multiple_of((i * per + e) * HD, HD), HD)
            out_ref[:, at] = o[e]
        return carry

    def hist_copy(buf, ss, rs, axis, me, k):
        return remote(buf.at[me], buf.at[me], ss.at[k], rs.at[me], {axis: (me + k) % 16})

    def hist_start(buf, ss, rs, axis, me):
        def start(k, carry):
            hist_copy(buf, ss, rs, axis, me, k).start()
            return carry

        lax.fori_loop(1, 16, start, 0)

    def hist_total(buf, ss, rs, axis, me):
        def wait(k, carry):
            s = (me + k) % 16
            remote(buf.at[s], buf.at[s], ss.at[k], rs.at[s], {axis: s}).wait_recv()
            return carry

        lax.fori_loop(1, 16, wait, 0)
        return jnp.sum(buf[...], axis=0)

    hist_start(hist_a, ha_ss, ha_rs, "dp", dp)
    lax.fori_loop(0, HALF, heads, 0, unroll=2)
    hist_b[ctx] = hist_total(hist_a, ha_ss, ha_rs, "dp", dp)
    hist_start(hist_b, hb_ss, hb_rs, "ctx", ctx)
    lax.fori_loop(HALF, HQ // PER, heads, 0, unroll=2)
    hist_ref[...] = hist_total(hist_b, hb_ss, hb_rs, "ctx", ctx)

    def drain(k, carry):
        k_copy(k).wait_send()
        v_copy(k).wait_send()
        q_copy(k).wait_send()
        hist_copy(hist_a, ha_ss, ha_rs, "dp", dp, k).wait_send()
        hist_copy(hist_b, hb_ss, hb_rs, "ctx", ctx, k).wait_send()
        return carry

    lax.fori_loop(1, 16, drain, 0)

    @pl.when(ctx > 0)
    def _():
        seg_copy.wait_send()

    def counted(low, high):
        total = jnp.int32(0)
        for c, steps in enumerate(ROUTES):
            total += jnp.where(ctx == c, sum(low <= n < high for n in steps), 0)
        return total

    k_sends = counted(0, 256)

    def drain_items(item):
        def body(slot, carry):
            item_copy(item, ctx, slot).wait_send()
            return carry

        return body

    lax.fori_loop(0, k_sends, drain_items(0), 0)
    lax.fori_loop(k_sends, k_sends + counted(256, 512), drain_items(16), 0)


def local(roll_query, roll_keys, roll_values, pack_dest, segment_ids, reward_bins, reward_weight):
    vmem = pl.BlockSpec(memory_space=pltpu.VMEM)
    hbm = pl.BlockSpec(memory_space=pltpu.HBM)
    bf16, f32, i32 = jnp.bfloat16, jnp.float32, jnp.int32
    dma = pltpu.SemaphoreType.DMA
    most = max(sum(n >= 0 for n in steps) for steps in ROUTES)
    out, hist = pl.pallas_call(
        kernel,
        out_shape=(pltpu.VMEM((TQ, HQ * HD), bf16), pltpu.VMEM((1, BINS), f32)),
        in_specs=[hbm] * 7,
        out_specs=(vmem, vmem),
        scratch_shapes=[
            pltpu.SMEM((16, NB), i32),
            pltpu.SMEM((1, SEGS), i32),
            pltpu.VMEM((1, 1, TQ), i32),
            pltpu.VMEM((NB, BLK, HQ * HD), bf16),
            pltpu.VMEM((NB, BLK, HK * HD), bf16),
            pltpu.VMEM((NB, BLK, HK * HD), bf16),
            pltpu.VMEM((HQ, HD), f32),
            pltpu.VMEM((16, BLK, HQ * HD), bf16),
            pltpu.VMEM((16, BLK, HQ * HD), bf16),
            pltpu.VMEM((16, BLK, HK * HD), bf16),
            pltpu.VMEM((16, BLK, HK * HD), bf16),
            pltpu.VMEM((16, BLK, HK * HD), bf16),
            pltpu.VMEM((16, BLK, HK * HD), bf16),
            pltpu.VMEM((HQ, TQ, HD), bf16),
            pltpu.VMEM((HK, GROUP * SEGS, HD), bf16),
            pltpu.VMEM((16, HK * TQ + 16, HD), bf16),
            pltpu.VMEM((16, HK * TQ, HD), bf16),
            pltpu.VMEM((1, TQ), i32),
            pltpu.VMEM((TQ, WIN * TQ), f32),
            pltpu.VMEM((SEGS, WIN * TQ), f32),
            pltpu.VMEM((16, 1, BINS), f32),
            pltpu.VMEM((16, 1, BINS), f32),
            dma((7,)), dma((16,)), dma((16,)), dma((16,)), dma((16,)), dma((16,)), dma((16,)),
            dma, dma, dma((most,)), dma((32,)), dma((16,)), dma((16,)), dma((16,)), dma((16,)),
            pltpu.SemaphoreType.REGULAR((4,)),
        ],
        compiler_params=pltpu.CompilerParams(
            collective_id=0, has_side_effects=True, vmem_limit_bytes=56 * 1024 * 1024
        ),
    )(
        pack_dest,
        reward_bins,
        roll_query.reshape(NB, BLK, HQ * HD),
        roll_keys.reshape(NB, BLK, HK * HD),
        roll_values.reshape(NB, BLK, HK * HD),
        segment_ids.reshape(1, 1, TQ),
        reward_weight.reshape(HQ, HD),
    )
    return out.reshape(1, TQ, HQ * HD), hist.reshape(BINS)


def solution(mesh):
    in_specs = (
        P("dp", "ctx", None),
        P("dp", "ctx", None),
        P("dp", "ctx", None),
        P(None, "ctx"),
        P("dp", "ctx"),
        P("dp", None),
        P(),
    )
    out_specs = (P("dp", "ctx", None), P())
    return jax.shard_map(local, mesh=mesh, in_specs=in_specs, out_specs=out_specs, check_vma=False)
```

```python
import functools
import math

import jax
import jax.numpy as jnp
from jax import lax
from jax.experimental import pallas as pl
from jax.experimental.pallas import tpu as pltpu
from jax.sharding import PartitionSpec as P

HQ = 32
HK = 4
HD = 128
TQ = 128
BLK = 8
NB = 16
SEGS = 16
BINS = 512
GROUP = HQ // HK
WIN = 9
PER = 2
HALF = 8
NEG = -1e30
SCALE = math.log2(math.e) / math.sqrt(HD)
MESH = pl.DeviceIdType.MESH

ROUTES = (
    (264, 7, 1, 263, 257, -18, 8, 279, -2, -7, 104, 23, -19, 295, -3, 24, -22, 39, 337, -20, 344, 311, 312),
    (272, 281, 18, 16, 274, -1, -19, 297, 288, 2, -17, -3, 32, 25, 258, -20, 304, 313, -22, 345),
    (35, 42, 289, 291, 33, -20, -2, 314, 19, 305, -18, -21, 275, 330, -1, 3, -6, -17, 90, 259, -7, 106),
    (306, 52, 59, 308, -21, -3, 322, 331, 36, -19, -6, 82, 292, 91, -2, 20, -7, -18, 98, 107, 276, -1, 315, -17),
    (323, 76, 325, 69, -4, -6, 83, 92, 53, -20, -7, 99, 108, 309, -3, 37, -19, -24, 380, 293, -2, -1, 332, -18, -17),
    (84, 349, 342, 86, -7, -21, 100, 109, 326, -5, -24, 372, 381, 70, -4, 54, -1, -20, 4, 93, 310, -17, -3, 260, 38, -18, -19, -2),
    (101, 366, 103, 359, -24, -22, 373, 382, 343, -6, -1, 5, 110, 87, -21, -17, 261, 327, -5, -18, 277, 71, -4, -2, 21, 55, -20, -19, -3),
    (374, 127, -1, -7, 6, 96, 383, -17, -23, 262, 367, -18, -22, 278, 336, -2, -6, 22, 95, -19, -21, 294, -3, -5, -20, -4),
    (393, 143, 137, 399, -10, 159, -17, -26, 415, -11, -1, -8, 121, 175, -18, -7, -24, -19, 377, -3, 105, -2, -23, -4, 361, -22, -6, -21, -5, -20),
    (410, 152, 154, 408, -25, -11, 394, 168, -18, -9, 138, 280, -19, -3, 298, 296, 40, -2, -8, -4, 122, 56, -20, -24, -21, 378, 328, -7, -5, 72, -22, -23, -6),
    (169, 427, 171, -26, 411, -3, -10, 41, 155, -25, -20, -4, 57, 395, -9, 139, -21, -19, -5, 329, 73, -6, -8, -22, 123, 89, -7, -24, -23),
    (444, 188, -27, 428, -4, -11, 58, 172, -26, -21, -5, 412, 74, -10, 156, -6, -22, -25, 346, 396, -9, -7, -23, 362, -20, -24, -8),
    (205, 461, -28, 445, -5, -12, 75, 189, -27, -6, -22, 347, 429, -11, 173, -7, -23, -26, 363, 413, -9, -10, -24, 379, -8, -25, -21),
    (222, 478, -13, 206, -22, -29, 348, 462, -28, -7, -23, 446, 364, -12, -9, 190, 140, -24, -27, -8, 430, 124, -11, -6, -10, -26, -25),
    (239, 495, -14, 223, -23, -30, 365, -9, 479, -13, 141, -24, -8, 207, -29, 125, -10, 463, -7, -28, 157, -25, 447, -12, 397, -11, 191, -27, -26, 431),
    (-9, -15, 142, -8, -25, -31, 120, 126, -10, -14, 158, -24, 376, -26, -30, 398, -23, -11, -13, 360, 174, -29, 414, -6, 88, -28, -12, -27),
)
CUTS = (22, 20, 22, 24, 25, 28, 29, 26, 24, 27, 25, 24, 26, 26, 28, 26)


def remote(src, dst, send_sem, recv_sem, device_id):
    return pltpu.make_async_remote_copy(
        src_ref=src, dst_ref=dst, send_sem=send_sem, recv_sem=recv_sem, device_id=device_id, device_id_type=MESH
    )


def kernel(
    dest_hbm, bins_hbm, rq_hbm, rk_hbm, rv_hbm, seg_hbm, rw_hbm,
    out_ref, hist_ref,
    dest_ref, bins_ref, source, seg_ref, rq_ref, rk_ref, rv_ref, rw_ref, qsend, qrecv, ksend, krecv, vsend, vrecv, qs, qe, kbuf, vbuf, seg_next,
    bias, bias_end, hist_a, hist_b,
    in_sem, q_ss, q_rs, k_ss, k_rs, v_ss, v_rs, seg_ss, seg_rs, item_ss, item_rs,
    ha_ss, ha_rs, hb_ss, hb_rs, known,
):
    dp = lax.axis_index("dp")
    ctx = lax.axis_index("ctx")
    line = ctx // 8 * 8
    near = (line + (ctx + 1) % 8, line + (ctx + 7) % 8, (ctx + 8) % 16)
    loads = [
        pltpu.make_async_copy(src, dst, in_sem.at[i])
        for i, (src, dst) in enumerate(
            (
                (dest_hbm, dest_ref), (rk_hbm, rk_ref), (rv_hbm, rv_ref), (seg_hbm, seg_ref),
                (bins_hbm, bins_ref), (rq_hbm, rq_ref), (rw_hbm, rw_ref),
            )
        )
    ]
    barrier = pltpu.get_barrier_semaphore()

    def greet(k, carry):
        pl.semaphore_signal(barrier, inc=1, device_id={"dp": (dp + k) % 16}, device_id_type=MESH)
        return carry

    lax.fori_loop(1, 16, greet, 0, unroll=5)
    for to in near:
        pl.semaphore_signal(barrier, inc=1, device_id={"ctx": to}, device_id_type=MESH)

    @pl.when(ctx == 7)
    def _():
        pl.semaphore_signal(barrier, inc=1, device_id={"ctx": 8}, device_id_type=MESH)

    for load in loads:
        load.start()

    def fill(src, dst):
        def body(d, carry):
            inv = jnp.int32(0)
            for j in range(NB):
                inv = jnp.where(dest_ref[dp, j] == d, j, inv)
            dst[d] = src[inv]
            return carry

        lax.fori_loop(0, NB, body, 0)

    def exchange(send, recv, ss, rs):
        def copy(k):
            d = (dp + k) % 16
            return remote(send.at[d], recv.at[dp], ss.at[k], rs.at[dp], {"dp": d})

        def start(k, carry):
            copy(k).start()
            return carry

        def wait(k, carry):
            s = (dp + k) % 16
            remote(send.at[s], recv.at[s], ss.at[k], rs.at[s], {"dp": s}).wait_recv()
            return carry

        return copy, start, wait

    k_copy, k_start, k_wait = exchange(ksend, krecv, k_ss, k_rs)
    v_copy, v_start, v_wait = exchange(vsend, vrecv, v_ss, v_rs)
    q_copy, q_start, q_wait = exchange(qsend, qrecv, q_ss, q_rs)
    loads[0].wait()
    loads[1].wait()
    fill(rk_ref, ksend)
    loads[2].wait()
    fill(rv_ref, vsend)
    pl.semaphore_wait(barrier, 18 + jnp.where(ctx == 8, 1, 0))
    lax.fori_loop(1, 16, k_start, 0, unroll=5)
    lax.fori_loop(1, 16, v_start, 0)
    krecv[dp] = ksend[dp]
    vrecv[dp] = vsend[dp]

    def spread(r):
        for to in near:
            pl.semaphore_signal(known.at[r], inc=1, device_id={"ctx": to}, device_id_type=MESH)

    def heard(r):
        pl.semaphore_wait(known.at[r], 3)

    loads[3].wait()
    loads[4].wait()
    seg_copy = remote(seg_ref.at[0], seg_next, seg_ss, seg_rs, {"ctx": (ctx + 15) % 16})
    spread(0)

    @pl.when(ctx > 0)
    def _():
        seg_copy.start()

    loads[5].wait()
    fill(rq_ref, qsend)
    loads[6].wait()
    heard(0)
    spread(1)

    for j in range(NB):
        src = jnp.int32(0)
        for s in range(16):
            src = jnp.where(dest_ref[s, j] == dp, s, src)
        source[j] = src

    def rows_of(recv, jj):
        top = recv[source[2 * jj]].astype(jnp.float32)
        low = recv[source[2 * jj + 1]].astype(jnp.float32)
        return jnp.concatenate([top, low], axis=0).astype(jnp.bfloat16)

    def pack(recv, buf):
        def body(jj, carry):
            rows = rows_of(recv, jj)
            for g in range(HK):
                at = pl.ds(pl.multiple_of(g * TQ + jj * 16, 16), 16)
                buf[ctx, at, :] = rows[:, g * HD : (g + 1) * HD]
            return carry

        lax.fori_loop(0, NB // 2, body, 0, unroll=4)

    def item_copy(item, to, slot):
        buf = (kbuf, vbuf)[item // 16].at[item % 16]
        return remote(buf, buf, item_ss.at[slot], item_rs.at[item], {"ctx": to})

    slots = []
    for steps in ROUTES:
        k_sends = [n for n in steps if 0 <= n < 256]
        v_sends = [n for n in steps if n >= 256]
        slots.append({n: i for i, n in enumerate(k_sends + v_sends)})

    def run_steps(c, steps):
        for n in steps:
            if n < 0:
                item_copy(-1 - n, ctx, 0).wait_recv()
            else:
                item_copy(n // 16, n % 16, slots[c][n]).start()

    first = [next((i for i, n in enumerate(steps) if n < 0), len(steps)) for steps in ROUTES]
    seg_row = seg_ref[0]
    kbuf[ctx, HK * TQ :, :] = jnp.broadcast_to(seg_row.astype(jnp.float32), (16, TQ)).astype(jnp.bfloat16)
    lax.fori_loop(1, 16, k_wait, 0, unroll=5)
    pack(krecv, kbuf)
    for c, steps in enumerate(ROUTES):
        @pl.when(ctx == c)
        def _():
            run_steps(c, [n for n in steps[: first[c]] if n < 256])

    lax.fori_loop(1, 16, v_wait, 0)
    pack(vrecv, vbuf)
    for c, steps in enumerate(ROUTES):
        @pl.when(ctx == c)
        def _():
            run_steps(c, [n for n in steps[: first[c]] if n >= 256])

    lax.fori_loop(1, 16, q_start, 0)
    qrecv[dp] = qsend[dp]
    heard(1)
    spread(2)
    for c, steps in enumerate(ROUTES):
        @pl.when(ctx == c)
        def _():
            for b in range(c + 1, WIN):
                if -1 - b not in steps:
                    kbuf[b] = jnp.zeros((HK * TQ + 16, HD), jnp.bfloat16)
                if -1 - (16 + b) not in steps:
                    vbuf[b] = jnp.zeros((HK * TQ, HD), jnp.bfloat16)
            run_steps(c, steps[first[c] : CUTS[c]])

    heard(2)
    spread(3)
    lax.fori_loop(1, 16, q_wait, 0)

    def pack_q(jj, carry):
        rows = rows_of(qrecv, jj)
        at = pl.ds(pl.multiple_of(jj * 16, 16), 16)
        for h in range(HQ):
            qs[h, at, :] = rows[:, h * HD : (h + 1) * HD]
        return carry

    lax.fori_loop(0, NB // 2, pack_q, 0)

    @pl.when(ctx < 15)
    def _():
        remote(seg_ref.at[0], seg_next, seg_ss, seg_rs, {"ctx": ctx}).wait_recv()

    def column(row):
        return jnp.transpose(jnp.broadcast_to(row.astype(jnp.float32), (TQ, TQ)))

    lane = lax.broadcasted_iota(jnp.int32, (TQ, TQ), 1)
    sub = lax.broadcasted_iota(jnp.int32, (TQ, TQ), 0)
    seg_col = column(seg_row)
    base = jnp.maximum(ctx - (WIN - 1), 0)
    wide = (SEGS, TQ)
    lane_row = lane[:1]
    end_lane = lax.broadcasted_iota(jnp.int32, wide, 1).astype(jnp.float32)
    end_seg = lax.broadcasted_iota(jnp.int32, wide, 0)
    following = jnp.where(
        lane_row == TQ - 1, pltpu.roll(seg_next[...], TQ - 1, 1), pltpu.roll(seg_row, TQ - 1, 1)
    )
    is_end = (following != seg_row) | ((lane_row == TQ - 1) & (ctx == 15))
    pick = jnp.where((seg_row == end_seg) & is_end, 1.0, 0.0)
    end_pos = jnp.sum(pick * end_lane, axis=1, keepdims=True)
    has_end = jnp.sum(pick, axis=1, keepdims=True)
    pick = pick.astype(jnp.bfloat16)
    for h in range(HQ):
        rows = jnp.dot(pick, qs[h], preferred_element_type=jnp.float32).astype(jnp.bfloat16)
        qe[h // GROUP, (h % GROUP) * SEGS : (h % GROUP + 1) * SEGS] = rows

    for c, steps in enumerate(ROUTES):
        @pl.when(ctx == c)
        def _():
            run_steps(c, steps[CUTS[c] :])

    heard(3)
    end_seg_f = end_seg.astype(jnp.float32)
    for w in range(WIN):
        keys = kbuf[base + w, HK * TQ :, :].astype(jnp.float32)
        offset = (base + w - ctx) * TQ
        at = slice(w * TQ, (w + 1) * TQ)
        ends = (keys == end_seg_f) & (end_lane + offset.astype(jnp.float32) <= end_pos)
        bias_end[:, at] = jnp.where(ends, 0.0, NEG)
        allowed = (seg_col == keys[:1]) & (offset + lane <= sub)
        bias[:, at] = jnp.where(allowed, 0.0, NEG)

    def attend(q, g, mask, per, rows):
        part = pl.ds(pl.multiple_of(g * TQ, TQ), TQ)
        k = kbuf[pl.ds(base, WIN), part, :].reshape(WIN * TQ, HD)
        v = vbuf[pl.ds(base, WIN), part, :].reshape(WIN * TQ, HD)
        s = lax.dot_general(q, k, (((1,), (1,)), ((), ())), preferred_element_type=jnp.float32)
        s = (s * SCALE).reshape(per, rows, WIN * TQ) + mask[None]
        top = jnp.max(s, axis=-1, keepdims=True)
        p = jnp.exp2(s - top)
        total = jnp.sum(p, axis=-1, keepdims=True)
        pb = p.astype(jnp.bfloat16).reshape(per * rows, WIN * TQ)
        o = jnp.dot(pb, v, preferred_element_type=jnp.float32).reshape(per, rows, HD)
        return (o / total).astype(jnp.bfloat16)

    terms = jnp.zeros((SEGS, HD), jnp.float32)
    for g in range(HK):
        o = attend(qe[g], g, bias_end[...], GROUP, SEGS)
        for j in range(GROUP):
            h = g * GROUP + j
            terms += o[j].astype(jnp.float32) * rw_ref[h : h + 1, :]
    reward = jnp.where(has_end > 0.5, jnp.sum(terms, axis=1, keepdims=True), 0.0)
    bin_seg = lax.broadcasted_iota(jnp.int32, (SEGS, BINS), 0)
    bin_lane = lax.broadcasted_iota(jnp.int32, (SEGS, BINS), 1)
    bin_of = jnp.zeros((SEGS, BINS), jnp.int32)
    for s in range(SEGS):
        bin_of = jnp.where(bin_seg == s, bins_ref[0, s], bin_of)
    hist_a[dp] = jnp.sum(jnp.where(bin_of == bin_lane, reward, 0.0), axis=0, keepdims=True)

    def heads(i, carry):
        per = PER
        o = attend(qs[pl.ds(i * per, per)].reshape(per * TQ, HD), i // (GROUP // per), bias[...], per, TQ)
        for e in range(per):
            at = pl.ds(pl.multiple_of((i * per + e) * HD, HD), HD)
            out_ref[:, at] = o[e]
        return carry

    def hist_copy(buf, ss, rs, axis, me, k):
        return remote(buf.at[me], buf.at[me], ss.at[k], rs.at[me], {axis: (me + k) % 16})

    def hist_start(buf, ss, rs, axis, me):
        def start(k, carry):
            hist_copy(buf, ss, rs, axis, me, k).start()
            return carry

        lax.fori_loop(1, 16, start, 0, unroll=5)

    def hist_total(buf, ss, rs, axis, me):
        def wait(k, carry):
            s = (me + k) % 16
            remote(buf.at[s], buf.at[s], ss.at[k], rs.at[s], {axis: s}).wait_recv()
            return carry

        lax.fori_loop(1, 16, wait, 0, unroll=5)
        return jnp.sum(buf[...], axis=0)

    hist_start(hist_a, ha_ss, ha_rs, "dp", dp)
    lax.fori_loop(0, HALF, heads, 0, unroll=2)
    hist_b[ctx] = hist_total(hist_a, ha_ss, ha_rs, "dp", dp)
    hist_start(hist_b, hb_ss, hb_rs, "ctx", ctx)
    lax.fori_loop(HALF, HQ // PER, heads, 0, unroll=2)
    def drain(k, carry):
        k_copy(k).wait_send()
        v_copy(k).wait_send()
        q_copy(k).wait_send()
        hist_copy(hist_a, ha_ss, ha_rs, "dp", dp, k).wait_send()
        return carry

    lax.fori_loop(1, 16, drain, 0)

    @pl.when(ctx > 0)
    def _():
        seg_copy.wait_send()

    def counted(low, high):
        total = jnp.int32(0)
        for c, steps in enumerate(ROUTES):
            total += jnp.where(ctx == c, sum(low <= n < high for n in steps), 0)
        return total

    k_sends = counted(0, 256)

    def drain_items(item):
        def body(slot, carry):
            item_copy(item, ctx, slot).wait_send()
            return carry

        return body

    lax.fori_loop(0, k_sends, drain_items(0), 0)
    lax.fori_loop(k_sends, k_sends + counted(256, 512), drain_items(16), 0)

    hist_ref[...] = hist_total(hist_b, hb_ss, hb_rs, "ctx", ctx)

    def drain_last(k, carry):
        hist_copy(hist_b, hb_ss, hb_rs, "ctx", ctx, k).wait_send()
        return carry

    lax.fori_loop(1, 16, drain_last, 0, unroll=5)


def local(roll_query, roll_keys, roll_values, pack_dest, segment_ids, reward_bins, reward_weight):
    vmem = pl.BlockSpec(memory_space=pltpu.VMEM)
    hbm = pl.BlockSpec(memory_space=pltpu.HBM)
    bf16, f32, i32 = jnp.bfloat16, jnp.float32, jnp.int32
    dma = pltpu.SemaphoreType.DMA
    most = max(sum(n >= 0 for n in steps) for steps in ROUTES)
    out, hist = pl.pallas_call(
        kernel,
        out_shape=(pltpu.VMEM((TQ, HQ * HD), bf16), pltpu.VMEM((1, BINS), f32)),
        in_specs=[hbm] * 7,
        out_specs=(vmem, vmem),
        scratch_shapes=[
            pltpu.SMEM((16, NB), i32),
            pltpu.SMEM((1, SEGS), i32),
            pltpu.SMEM((NB,), i32),
            pltpu.VMEM((1, 1, TQ), i32),
            pltpu.VMEM((NB, BLK, HQ * HD), bf16),
            pltpu.VMEM((NB, BLK, HK * HD), bf16),
            pltpu.VMEM((NB, BLK, HK * HD), bf16),
            pltpu.VMEM((HQ, HD), f32),
            pltpu.VMEM((16, BLK, HQ * HD), bf16),
            pltpu.VMEM((16, BLK, HQ * HD), bf16),
            pltpu.VMEM((16, BLK, HK * HD), bf16),
            pltpu.VMEM((16, BLK, HK * HD), bf16),
            pltpu.VMEM((16, BLK, HK * HD), bf16),
            pltpu.VMEM((16, BLK, HK * HD), bf16),
            pltpu.VMEM((HQ, TQ, HD), bf16),
            pltpu.VMEM((HK, GROUP * SEGS, HD), bf16),
            pltpu.VMEM((16, HK * TQ + 16, HD), bf16),
            pltpu.VMEM((16, HK * TQ, HD), bf16),
            pltpu.VMEM((1, TQ), i32),
            pltpu.VMEM((TQ, WIN * TQ), f32),
            pltpu.VMEM((SEGS, WIN * TQ), f32),
            pltpu.VMEM((16, 1, BINS), f32),
            pltpu.VMEM((16, 1, BINS), f32),
            dma((7,)), dma((16,)), dma((16,)), dma((16,)), dma((16,)), dma((16,)), dma((16,)),
            dma, dma, dma((most,)), dma((32,)), dma((16,)), dma((16,)), dma((16,)), dma((16,)),
            pltpu.SemaphoreType.REGULAR((4,)),
        ],
        compiler_params=pltpu.CompilerParams(
            collective_id=0, has_side_effects=True, vmem_limit_bytes=56 * 1024 * 1024
        ),
    )(
        pack_dest,
        reward_bins,
        roll_query.reshape(NB, BLK, HQ * HD),
        roll_keys.reshape(NB, BLK, HK * HD),
        roll_values.reshape(NB, BLK, HK * HD),
        segment_ids.reshape(1, 1, TQ),
        reward_weight.reshape(HQ, HD),
    )
    return out.reshape(1, TQ, HQ * HD), hist.reshape(BINS)


def solution(mesh):
    in_specs = (
        P("dp", "ctx", None),
        P("dp", "ctx", None),
        P("dp", "ctx", None),
        P(None, "ctx"),
        P("dp", "ctx"),
        P("dp", None),
        P(),
    )
    out_specs = (P("dp", "ctx", None), P())
    return jax.shard_map(local, mesh=mesh, in_specs=in_specs, out_specs=out_specs, check_vma=False)
```

```python
import functools
import math

import jax
import jax.numpy as jnp
from jax import lax
from jax.experimental import pallas as pl
from jax.experimental.pallas import tpu as pltpu
from jax.sharding import PartitionSpec as P

HQ = 32
HK = 4
HD = 128
TQ = 128
BLK = 8
NB = 16
SEGS = 16
BINS = 512
GROUP = HQ // HK
WIN = 9
PER = 2
HALF = 8
NEG = -1e30
SCALE = math.log2(math.e) / math.sqrt(HD)
MESH = pl.DeviceIdType.MESH

ROUTES = (
    (264, 7, 1, 263, 257, -18, 8, 279, -2, -7, 104, 23, -19, 295, -3, 24, -22, 39, 337, -20, 344, 311, 312),
    (272, 281, 18, 16, 274, -1, -19, 297, 288, 2, -17, -3, 32, 25, 258, -20, 304, 313, -22, 345),
    (35, 42, 289, 291, 33, -20, -2, 314, 19, 305, -18, -21, 275, 330, -1, 3, -6, -17, 90, 259, -7, 106),
    (306, 52, 59, 308, -21, -3, 322, 331, 36, -19, -6, 82, 292, 91, -2, 20, -7, -18, 98, 107, 276, -1, 315, -17),
    (323, 76, 325, 69, -4, -6, 83, 92, 53, -20, -7, 99, 108, 309, -3, 37, -19, -24, 380, 293, -2, -1, 332, -18, -17),
    (84, 349, 342, 86, -7, -21, 100, 109, 326, -5, -24, 372, 381, 70, -4, 54, -1, -20, 4, 93, 310, -17, -3, 260, 38, -18, -19, -2),
    (101, 366, 103, 359, -24, -22, 373, 382, 343, -6, -1, 5, 110, 87, -21, -17, 261, 327, -5, -18, 277, 71, -4, -2, 21, 55, -20, -19, -3),
    (374, 127, -1, -7, 6, 96, 383, -17, -23, 262, 367, -18, -22, 278, 336, -2, -6, 22, 95, -19, -21, 294, -3, -5, -20, -4),
    (393, 143, 137, 399, -10, 159, -17, -26, 415, -11, -1, -8, 121, 175, -18, -7, -24, -19, 377, -3, 105, -2, -23, -4, 361, -22, -6, -21, -5, -20),
    (410, 152, 154, 408, -25, -11, 394, 168, -18, -9, 138, 280, -19, -3, 298, 296, 40, -2, -8, -4, 122, 56, -20, -24, -21, 378, 328, -7, -5, 72, -22, -23, -6),
    (169, 427, 171, -26, 411, -3, -10, 41, 155, -25, -20, -4, 57, 395, -9, 139, -21, -19, -5, 329, 73, -6, -8, -22, 123, 89, -7, -24, -23),
    (444, 188, -27, 428, -4, -11, 58, 172, -26, -21, -5, 412, 74, -10, 156, -6, -22, -25, 346, 396, -9, -7, -23, 362, -20, -24, -8),
    (205, 461, -28, 445, -5, -12, 75, 189, -27, -6, -22, 347, 429, -11, 173, -7, -23, -26, 363, 413, -9, -10, -24, 379, -8, -25, -21),
    (222, 478, -13, 206, -22, -29, 348, 462, -28, -7, -23, 446, 364, -12, -9, 190, 140, -24, -27, -8, 430, 124, -11, -6, -10, -26, -25),
    (239, 495, -14, 223, -23, -30, 365, -9, 479, -13, 141, -24, -8, 207, -29, 125, -10, 463, -7, -28, 157, -25, 447, -12, 397, -11, 191, -27, -26, 431),
    (-9, -15, 142, -8, -25, -31, 120, 126, -10, -14, 158, -24, 376, -26, -30, 398, -23, -11, -13, 360, 174, -29, 414, -6, 88, -28, -12, -27),
)
CUTS = (22, 20, 22, 24, 25, 28, 29, 26, 24, 27, 25, 24, 26, 26, 28, 26)


def remote(src, dst, send_sem, recv_sem, device_id):
    return pltpu.make_async_remote_copy(
        src_ref=src, dst_ref=dst, send_sem=send_sem, recv_sem=recv_sem, device_id=device_id, device_id_type=MESH
    )


def kernel(
    dest_hbm, bins_hbm, rq_hbm, rk_hbm, rv_hbm, seg_hbm, rw_hbm,
    out_ref, hist_ref,
    dest_ref, bins_ref, source, seg_ref, rq_ref, rk_ref, rv_ref, rw_ref, qsend, qrecv, ksend, krecv, vsend, vrecv, qs, qe, kbuf, vbuf, seg_next,
    bias, bias_end, hist_a, hist_b,
    in_sem, q_ss, q_rs, k_ss, k_rs, v_ss, v_rs, seg_ss, seg_rs, item_ss, item_rs,
    ha_ss, ha_rs, hb_ss, hb_rs, known,
):
    dp = lax.axis_index("dp")
    ctx = lax.axis_index("ctx")
    line = ctx // 8 * 8
    near = (line + (ctx + 1) % 8, line + (ctx + 7) % 8, (ctx + 8) % 16)
    loads = [
        pltpu.make_async_copy(src, dst, in_sem.at[i])
        for i, (src, dst) in enumerate(
            (
                (dest_hbm, dest_ref), (rk_hbm, rk_ref), (rv_hbm, rv_ref), (seg_hbm, seg_ref),
                (bins_hbm, bins_ref), (rq_hbm, rq_ref), (rw_hbm, rw_ref),
            )
        )
    ]
    barrier = pltpu.get_barrier_semaphore()

    def greet(k, carry):
        pl.semaphore_signal(barrier, inc=1, device_id={"dp": (dp + k) % 16}, device_id_type=MESH)
        return carry

    lax.fori_loop(1, 16, greet, 0, unroll=5)
    for to in near:
        pl.semaphore_signal(barrier, inc=1, device_id={"ctx": to}, device_id_type=MESH)

    @pl.when(ctx == 7)
    def _():
        pl.semaphore_signal(barrier, inc=1, device_id={"ctx": 8}, device_id_type=MESH)

    for load in loads:
        load.start()

    def fill(src, dst):
        def body(d, carry):
            inv = jnp.int32(0)
            for j in range(NB):
                inv = jnp.where(dest_ref[dp, j] == d, j, inv)
            dst[d] = src[inv]
            return carry

        lax.fori_loop(0, NB, body, 0)

    def exchange(send, recv, ss, rs):
        def copy(k):
            d = (dp + k) % 16
            return remote(send.at[d], recv.at[dp], ss.at[k], rs.at[dp], {"dp": d})

        def start(k, carry):
            copy(k).start()
            return carry

        def wait(k, carry):
            s = (dp + k) % 16
            remote(send.at[s], recv.at[s], ss.at[k], rs.at[s], {"dp": s}).wait_recv()
            return carry

        return copy, start, wait

    k_copy, k_start, k_wait = exchange(ksend, krecv, k_ss, k_rs)
    v_copy, v_start, v_wait = exchange(vsend, vrecv, v_ss, v_rs)
    q_copy, q_start, q_wait = exchange(qsend, qrecv, q_ss, q_rs)
    loads[0].wait()
    loads[1].wait()
    fill(rk_ref, ksend)
    loads[2].wait()
    fill(rv_ref, vsend)
    pl.semaphore_wait(barrier, 18 + jnp.where(ctx == 8, 1, 0))
    lax.fori_loop(1, 16, k_start, 0, unroll=5)
    lax.fori_loop(1, 16, v_start, 0, unroll=5)
    krecv[dp] = ksend[dp]
    vrecv[dp] = vsend[dp]

    def spread(r):
        for to in near:
            pl.semaphore_signal(known.at[r], inc=1, device_id={"ctx": to}, device_id_type=MESH)

    def heard(r):
        pl.semaphore_wait(known.at[r], 3)

    loads[3].wait()
    loads[4].wait()
    seg_copy = remote(seg_ref.at[0], seg_next, seg_ss, seg_rs, {"ctx": (ctx + 15) % 16})
    spread(0)

    @pl.when(ctx > 0)
    def _():
        seg_copy.start()

    loads[5].wait()
    fill(rq_ref, qsend)
    loads[6].wait()
    heard(0)
    spread(1)

    for j in range(NB):
        src = jnp.int32(0)
        for s in range(16):
            src = jnp.where(dest_ref[s, j] == dp, s, src)
        source[j] = src

    def rows_of(recv, jj):
        top = recv[source[2 * jj]].astype(jnp.float32)
        low = recv[source[2 * jj + 1]].astype(jnp.float32)
        return jnp.concatenate([top, low], axis=0).astype(jnp.bfloat16)

    def pack(recv, buf):
        def body(jj, carry):
            rows = rows_of(recv, jj)
            for g in range(HK):
                at = pl.ds(pl.multiple_of(g * TQ + jj * 16, 16), 16)
                buf[ctx, at, :] = rows[:, g * HD : (g + 1) * HD]
            return carry

        lax.fori_loop(0, NB // 2, body, 0, unroll=4)

    def item_copy(item, to, slot):
        buf = (kbuf, vbuf)[item // 16].at[item % 16]
        return remote(buf, buf, item_ss.at[slot], item_rs.at[item], {"ctx": to})

    slots = []
    for steps in ROUTES:
        k_sends = [n for n in steps if 0 <= n < 256]
        v_sends = [n for n in steps if n >= 256]
        slots.append({n: i for i, n in enumerate(k_sends + v_sends)})

    def run_steps(c, steps):
        for n in steps:
            if n < 0:
                item_copy(-1 - n, ctx, 0).wait_recv()
            else:
                item_copy(n // 16, n % 16, slots[c][n]).start()

    first = [next((i for i, n in enumerate(steps) if n < 0), len(steps)) for steps in ROUTES]
    seg_row = seg_ref[0]
    kbuf[ctx, HK * TQ :, :] = jnp.broadcast_to(seg_row.astype(jnp.float32), (16, TQ)).astype(jnp.bfloat16)
    for c, steps in enumerate(ROUTES[: WIN - 1]):
        @pl.when(ctx == c)
        def _():
            for b in range(c + 1, WIN):
                if -1 - b not in steps:
                    kbuf[b] = jnp.zeros((HK * TQ + 16, HD), jnp.bfloat16)
                if -1 - (16 + b) not in steps:
                    vbuf[b] = jnp.zeros((HK * TQ, HD), jnp.bfloat16)

    lax.fori_loop(1, 16, k_wait, 0, unroll=5)
    pack(krecv, kbuf)
    for c, steps in enumerate(ROUTES):
        @pl.when(ctx == c)
        def _():
            run_steps(c, [n for n in steps[: first[c]] if n < 256])

    lax.fori_loop(1, 16, v_wait, 0, unroll=5)
    pack(vrecv, vbuf)
    for c, steps in enumerate(ROUTES):
        @pl.when(ctx == c)
        def _():
            run_steps(c, [n for n in steps[: first[c]] if n >= 256])

    lax.fori_loop(1, 16, q_start, 0, unroll=5)
    qrecv[dp] = qsend[dp]
    heard(1)
    spread(2)
    for c, steps in enumerate(ROUTES):
        @pl.when(ctx == c)
        def _():
            run_steps(c, steps[first[c] : CUTS[c]])

    heard(2)
    spread(3)
    lax.fori_loop(1, 16, q_wait, 0)

    def pack_q(jj, carry):
        rows = rows_of(qrecv, jj)
        at = pl.ds(pl.multiple_of(jj * 16, 16), 16)
        for h in range(HQ):
            qs[h, at, :] = rows[:, h * HD : (h + 1) * HD]
        return carry

    lax.fori_loop(0, NB // 2, pack_q, 0, unroll=2)

    @pl.when(ctx < 15)
    def _():
        remote(seg_ref.at[0], seg_next, seg_ss, seg_rs, {"ctx": ctx}).wait_recv()

    def column(row):
        return jnp.transpose(jnp.broadcast_to(row.astype(jnp.float32), (TQ, TQ)))

    lane = lax.broadcasted_iota(jnp.int32, (TQ, TQ), 1)
    sub = lax.broadcasted_iota(jnp.int32, (TQ, TQ), 0)
    seg_col = column(seg_row)
    base = jnp.maximum(ctx - (WIN - 1), 0)
    wide = (SEGS, TQ)
    lane_row = lane[:1]
    end_lane = lax.broadcasted_iota(jnp.int32, wide, 1).astype(jnp.float32)
    end_seg = lax.broadcasted_iota(jnp.int32, wide, 0)
    following = jnp.where(
        lane_row == TQ - 1, pltpu.roll(seg_next[...], TQ - 1, 1), pltpu.roll(seg_row, TQ - 1, 1)
    )
    is_end = (following != seg_row) | ((lane_row == TQ - 1) & (ctx == 15))
    pick = jnp.where((seg_row == end_seg) & is_end, 1.0, 0.0)
    end_pos = jnp.sum(pick * end_lane, axis=1, keepdims=True)
    has_end = jnp.sum(pick, axis=1, keepdims=True)
    pick = pick.astype(jnp.bfloat16)
    for h in range(HQ):
        rows = jnp.dot(pick, qs[h], preferred_element_type=jnp.float32).astype(jnp.bfloat16)
        qe[h // GROUP, (h % GROUP) * SEGS : (h % GROUP + 1) * SEGS] = rows

    for c, steps in enumerate(ROUTES):
        @pl.when(ctx == c)
        def _():
            run_steps(c, steps[CUTS[c] :])

    heard(3)
    end_seg_f = end_seg.astype(jnp.float32)
    for w in range(WIN):
        keys = kbuf[base + w, HK * TQ :, :].astype(jnp.float32)
        offset = (base + w - ctx) * TQ
        at = slice(w * TQ, (w + 1) * TQ)
        ends = (keys == end_seg_f) & (end_lane + offset.astype(jnp.float32) <= end_pos)
        bias_end[:, at] = jnp.where(ends, 0.0, NEG)
        allowed = (seg_col == keys[:1]) & (offset + lane <= sub)
        bias[:, at] = jnp.where(allowed, 0.0, NEG)

    def attend(q, g, mask, per, rows):
        part = pl.ds(pl.multiple_of(g * TQ, TQ), TQ)
        k = kbuf[pl.ds(base, WIN), part, :].reshape(WIN * TQ, HD)
        v = vbuf[pl.ds(base, WIN), part, :].reshape(WIN * TQ, HD)
        s = lax.dot_general(q, k, (((1,), (1,)), ((), ())), preferred_element_type=jnp.float32)
        s = (s * SCALE).reshape(per, rows, WIN * TQ) + mask[None]
        top = jnp.max(s, axis=-1, keepdims=True)
        p = jnp.exp2(s - top)
        total = jnp.sum(p, axis=-1, keepdims=True)
        pb = p.astype(jnp.bfloat16).reshape(per * rows, WIN * TQ)
        o = jnp.dot(pb, v, preferred_element_type=jnp.float32).reshape(per, rows, HD)
        return (o / total).astype(jnp.bfloat16)

    terms = jnp.zeros((SEGS, HD), jnp.float32)
    for g in range(HK):
        o = attend(qe[g], g, bias_end[...], GROUP, SEGS)
        for j in range(GROUP):
            h = g * GROUP + j
            terms += o[j].astype(jnp.float32) * rw_ref[h : h + 1, :]
    reward = jnp.where(has_end > 0.5, jnp.sum(terms, axis=1, keepdims=True), 0.0)
    bin_seg = lax.broadcasted_iota(jnp.int32, (SEGS, BINS), 0)
    bin_lane = lax.broadcasted_iota(jnp.int32, (SEGS, BINS), 1)
    bin_of = jnp.zeros((SEGS, BINS), jnp.int32)
    for s in range(SEGS):
        bin_of = jnp.where(bin_seg == s, bins_ref[0, s], bin_of)
    hist_a[dp] = jnp.sum(jnp.where(bin_of == bin_lane, reward, 0.0), axis=0, keepdims=True)

    def heads(i, carry):
        per = PER
        o = attend(qs[pl.ds(i * per, per)].reshape(per * TQ, HD), i // (GROUP // per), bias[...], per, TQ)
        for e in range(per):
            at = pl.ds(pl.multiple_of((i * per + e) * HD, HD), HD)
            out_ref[:, at] = o[e]
        return carry

    def hist_copy(buf, ss, rs, axis, me, k):
        return remote(buf.at[me], buf.at[me], ss.at[k], rs.at[me], {axis: (me + k) % 16})

    def hist_start(buf, ss, rs, axis, me):
        def start(k, carry):
            hist_copy(buf, ss, rs, axis, me, k).start()
            return carry

        lax.fori_loop(1, 16, start, 0, unroll=5)

    def hist_total(buf, ss, rs, axis, me):
        def wait(k, carry):
            s = (me + k) % 16
            remote(buf.at[s], buf.at[s], ss.at[k], rs.at[s], {axis: s}).wait_recv()
            return carry

        lax.fori_loop(1, 16, wait, 0, unroll=5)
        return jnp.sum(buf[...], axis=0)

    hist_start(hist_a, ha_ss, ha_rs, "dp", dp)
    lax.fori_loop(0, HALF, heads, 0, unroll=2)
    hist_b[ctx] = hist_total(hist_a, ha_ss, ha_rs, "dp", dp)
    hist_start(hist_b, hb_ss, hb_rs, "ctx", ctx)
    lax.fori_loop(HALF, HQ // PER, heads, 0, unroll=2)
    def drain(k, carry):
        k_copy(k).wait_send()
        v_copy(k).wait_send()
        q_copy(k).wait_send()
        hist_copy(hist_a, ha_ss, ha_rs, "dp", dp, k).wait_send()
        return carry

    lax.fori_loop(1, 16, drain, 0)

    @pl.when(ctx > 0)
    def _():
        seg_copy.wait_send()

    def counted(low, high):
        total = jnp.int32(0)
        for c, steps in enumerate(ROUTES):
            total += jnp.where(ctx == c, sum(low <= n < high for n in steps), 0)
        return total

    k_sends = counted(0, 256)

    def drain_items(item):
        def body(slot, carry):
            item_copy(item, ctx, slot).wait_send()
            return carry

        return body

    lax.fori_loop(0, k_sends, drain_items(0), 0)
    lax.fori_loop(k_sends, k_sends + counted(256, 512), drain_items(16), 0)

    hist_ref[...] = hist_total(hist_b, hb_ss, hb_rs, "ctx", ctx)

    def drain_last(k, carry):
        hist_copy(hist_b, hb_ss, hb_rs, "ctx", ctx, k).wait_send()
        return carry

    lax.fori_loop(1, 16, drain_last, 0, unroll=5)


def local(roll_query, roll_keys, roll_values, pack_dest, segment_ids, reward_bins, reward_weight):
    vmem = pl.BlockSpec(memory_space=pltpu.VMEM)
    hbm = pl.BlockSpec(memory_space=pltpu.HBM)
    bf16, f32, i32 = jnp.bfloat16, jnp.float32, jnp.int32
    dma = pltpu.SemaphoreType.DMA
    most = max(sum(n >= 0 for n in steps) for steps in ROUTES)
    out, hist = pl.pallas_call(
        kernel,
        out_shape=(pltpu.VMEM((TQ, HQ * HD), bf16), pltpu.VMEM((1, BINS), f32)),
        in_specs=[hbm] * 7,
        out_specs=(vmem, vmem),
        scratch_shapes=[
            pltpu.SMEM((16, NB), i32),
            pltpu.SMEM((1, SEGS), i32),
            pltpu.SMEM((NB,), i32),
            pltpu.VMEM((1, 1, TQ), i32),
            pltpu.VMEM((NB, BLK, HQ * HD), bf16),
            pltpu.VMEM((NB, BLK, HK * HD), bf16),
            pltpu.VMEM((NB, BLK, HK * HD), bf16),
            pltpu.VMEM((HQ, HD), f32),
            pltpu.VMEM((16, BLK, HQ * HD), bf16),
            pltpu.VMEM((16, BLK, HQ * HD), bf16),
            pltpu.VMEM((16, BLK, HK * HD), bf16),
            pltpu.VMEM((16, BLK, HK * HD), bf16),
            pltpu.VMEM((16, BLK, HK * HD), bf16),
            pltpu.VMEM((16, BLK, HK * HD), bf16),
            pltpu.VMEM((HQ, TQ, HD), bf16),
            pltpu.VMEM((HK, GROUP * SEGS, HD), bf16),
            pltpu.VMEM((16, HK * TQ + 16, HD), bf16),
            pltpu.VMEM((16, HK * TQ, HD), bf16),
            pltpu.VMEM((1, TQ), i32),
            pltpu.VMEM((TQ, WIN * TQ), f32),
            pltpu.VMEM((SEGS, WIN * TQ), f32),
            pltpu.VMEM((16, 1, BINS), f32),
            pltpu.VMEM((16, 1, BINS), f32),
            dma((7,)), dma((16,)), dma((16,)), dma((16,)), dma((16,)), dma((16,)), dma((16,)),
            dma, dma, dma((most,)), dma((32,)), dma((16,)), dma((16,)), dma((16,)), dma((16,)),
            pltpu.SemaphoreType.REGULAR((4,)),
        ],
        compiler_params=pltpu.CompilerParams(
            collective_id=0, has_side_effects=True, vmem_limit_bytes=56 * 1024 * 1024
        ),
    )(
        pack_dest,
        reward_bins,
        roll_query.reshape(NB, BLK, HQ * HD),
        roll_keys.reshape(NB, BLK, HK * HD),
        roll_values.reshape(NB, BLK, HK * HD),
        segment_ids.reshape(1, 1, TQ),
        reward_weight.reshape(HQ, HD),
    )
    return out.reshape(1, TQ, HQ * HD), hist.reshape(BINS)


def solution(mesh):
    in_specs = (
        P("dp", "ctx", None),
        P("dp", "ctx", None),
        P("dp", "ctx", None),
        P(None, "ctx"),
        P("dp", "ctx"),
        P("dp", None),
        P(),
    )
    out_specs = (P("dp", "ctx", None), P())
    return jax.shard_map(local, mesh=mesh, in_specs=in_specs, out_specs=out_specs, check_vma=False)
```
